128 devices in a mesh: group: 2 (over x_hi), dev: 64 (over z, x_lo, y, core).
Axes of the slice: x: 4 (x_hi: 2, x_lo: 2; x = x_hi * 2 + x_lo), y: 4, z: 4, core: 2. Of those that a mesh axis runs over, the one named last changes fastest.
Arguments:
- query_latent: bfloat16 [512, 128, 512], P(('group', 'dev')), may hold values from -100 to 100
- query_rope: bfloat16 [512, 128, 64], P(('group', 'dev')), may hold values from -3 to 3
- cache_latent: bfloat16 [512, 2048, 512], P(('group', 'dev')), may hold values from -6 to 6
- cache_rope: bfloat16 [512, 64, 2048], P(('group', 'dev')), may hold values from -6 to 6
- lengths: int32 [512], P(('group', 'dev')), may hold values from 256 to 2048
- value_up: bfloat16 [128, 512, 128], P('dev'), may hold values from -0.25 to 0.25
- out_proj: bfloat16 [16384, 7168], P('dev'), may hold values from -0.046875 to 0.046875
- residual: bfloat16 [512, 7168], P(('group', 'dev')), may hold values from -6 to 6
- norm_gain: float32 [7168], replicated, may hold values from 0.25 to 1.75
- expert_ids: int32 [512, 8], P(('group', 'dev')), may hold values from 0 to 31, all different within a row; in each aligned block of 4 rows (0 to 3, 4 to 7, ...) at most 2 rows name the same one
- gate_values: float32 [512, 8], P(('group', 'dev')), may hold values from 0.1 to 1
- w_gate: bfloat16 [64, 7168, 512], P('dev', None, 'group'), may hold values from -0.0625 to 0.0625
- w_up: bfloat16 [64, 7168, 512], P('dev', None, 'group'), may hold values from -0.0625 to 0.0625
- w_down: bfloat16 [64, 512, 7168], P('dev', 'group'), may hold values from -0.1875 to 0.1875
Outputs:
- layer_out: bfloat16 [512, 7168], P(('group', 'dev'))
The draws below stay inside these ranges and needn't reach their ends.
Inputs may be any that keep to these rules, and one draw needn't show every extreme that they name: `expert_ids`: each row names 8 different experts. Among the rows of one device no expert is named by more than 2 rows, and in every draw some expert is named by exactly 2 rows of some device.
All inputs are finite; a program needn't handle non-finite values.
Results may differ from the reference program's by a relative error of at most 0.008.
Values may be sent and summed in bfloat16 or wider, within the bound.
A program may use at most 128 MiB of HBM per device.

```python
import math
import jax
import jax.numpy as jnp
import numpy as np
from jax import lax

D = 7168
HEADS = 128
LATENT = 512
ROPE = 64
VHEAD = 128
FFW = 1024
TOP = 8
CTX = 2048
TOK_DEV = 4
EXPERTS = 32
CAP = 2
TOKENS = 512
N_GROUP = 2
N_DEV = 64


def shared_latents(key):
    base_key = jax.random.fold_in(key, 4242)
    cache_key, query_key = jax.random.split(base_key, 2)
    cache_draw = jnp.clip(jax.random.normal(cache_key, (TOKENS, CTX, LATENT), jnp.float32), -6.0, 6.0)
    query_draw = jnp.clip(0.5 * jax.random.normal(query_key, (TOKENS, HEADS, LATENT), jnp.float32), -3.0, 3.0)
    return (cache_draw, query_draw)


def draw_cache_latent(key, part):
    return shared_latents(key)[0].astype(jnp.bfloat16)


def draw_query_latent(key, part):
    return shared_latents(key)[1].astype(jnp.bfloat16)


def plant(result, rng, low, top_value):
    longest = result.shape.index(max(result.shape))
    spots = []
    for shift in (0, 1):
        where = [jax.random.randint(jax.random.fold_in(rng, axis), (), 0, length) for axis, length in enumerate(result.shape)]
        where[longest] = (where[longest] + shift) % result.shape[longest]
        spots.append(tuple(where))
    return result.at[spots[0]].set(low).at[spots[1]].set(top_value)


def levels(key, extent, cuts, smallest, largest):
    factor_of, own = 1.0, jax.random.fold_in(key, 6)
    for dim, parts in cuts:
        draws = jnp.exp(jax.random.uniform(jax.random.fold_in(own, dim), (parts,), jnp.float32, smallest / len(cuts), largest / len(cuts)))
        factor_of = factor_of * jnp.repeat(draws, extent[dim] // parts).reshape([-1 if axis == dim else 1 for axis in range(len(extent))])
    return factor_of


def routed_block(stream_key, own, number, rows, count, top, bound, lean):
    ranking = jax.random.permutation(stream_key, count)
    heavy_load, ordinary = shares(count, rows * top, bound, lean, True), shares(count, rows * top, bound, lean, False)
    places = jnp.arange(count)

    def named(tallies, offset_by):
        used = int((tallies > 0).sum())
        fixed = max(1, used // 4)
        passed = fixed + (places - fixed + offset_by * (used - fixed)) % max(1, count - fixed)
        return jnp.zeros((count,), jnp.int32).at[ranking[jnp.where(places < fixed, places, passed)]].set(jnp.asarray(tallies, jnp.int32))

    tallies = jnp.where(number % 4 == 0, named(heavy_load, number // 4), named(ordinary, number - number // 4 - 1))
    mixed = jax.random.permutation(jax.random.fold_in(own, 3), count)
    donor, receiver = mixed[0:count // 2 * 2:2], mixed[1:count // 2 * 2:2]
    slack = jnp.minimum(tallies[donor] - 1, bound - tallies[receiver]) // 2
    slack = jnp.where((donor == ranking[0]) | (receiver == ranking[0]) | (tallies[receiver] == 0), 0, jnp.maximum(slack, 0))
    passed = jax.random.randint(jax.random.fold_in(own, 4), (count // 2,), 0, 1 << 20) % (slack + 1)
    tallies = tallies.at[donor].add(-passed).at[receiver].add(passed)
    labels = jnp.searchsorted(jnp.cumsum(tallies), jnp.arange(rows * top), side="right").astype(jnp.int32)
    listing = labels.reshape(top, rows).T
    listing = listing[jax.random.permutation(jax.random.fold_in(own, 1), rows)]
    offset_by = jax.random.randint(jax.random.fold_in(own, 2), (rows, 1), 0, top)
    return jnp.take_along_axis(listing, (jnp.arange(top)[None, :] + offset_by) % top, axis=1)


def shares(number_of, total, most, slope, full):
    loads = [(1 << 20) // math.isqrt(grade ** slope) + 1 for grade in range(1, number_of + 1)]
    largest = most if full else min(most, max(-(-total // number_of), total * loads[0] // sum(loads)))
    least = 1 if total - largest >= number_of - 1 else 0
    holding, surplus = [largest] + [least] * (number_of - 1), total - largest - least * (number_of - 1)
    while surplus > 0:
        free = [i for i in range(1, number_of) if holding[i] < largest] or [i for i in range(1, number_of) if holding[i] < most]
        pool, left = sum([loads[i] for i in free]), surplus
        for i in free:
            extra = min(most - holding[i], max(1, left * loads[i] // pool), surplus)
            holding[i] = holding[i] + extra
            surplus = surplus - extra
    return np.array(holding)


def normal_values(rng, shape, width, limit, cuts=(), kind=jnp.bfloat16):
    entries = jax.random.normal(rng, shape, jnp.float32) * width
    if len(cuts) > 0:
        entries = levels(rng, shape, cuts, -0.22, 0.18) * entries
    return jnp.clip(entries, min=-limit, max=limit).astype(kind)


def setup_inputs(seed: int = 0) -> dict:
    seeds = jax.random.split(jax.random.key(seed), 15)
    query_latent = draw_query_latent(jax.random.fold_in(seeds[14], 71), 0)
    query_rope = normal_values(seeds[1], (TOKENS, HEADS, ROPE), 0.5, 3.0, ((0, 128),))
    cache_latent = draw_cache_latent(jax.random.fold_in(seeds[14], 71), 0)
    cache_rope = normal_values(seeds[3], (TOKENS, ROPE, CTX), 1.0, 6.0, ((0, 128),))
    lengths = plant(jax.random.randint(seeds[4], (TOKENS,), CTX // 8, CTX + 1), jax.random.fold_in(seeds[4], 1), CTX // 8, CTX).astype(jnp.int32)
    value_up = normal_values(seeds[5], (HEADS, LATENT, VHEAD), LATENT ** -0.5, 0.25, ((0, 64),))
    out_proj = normal_values(seeds[6], (HEADS * VHEAD, D), (HEADS * VHEAD) ** -0.5, 0.046875, ((0, 64),))
    residual = normal_values(seeds[7], (TOKENS, D), 1.0, 6.0, ((0, 128),))
    norm_gain = jnp.clip(1.0 + 0.15 * jax.random.normal(seeds[8], (D,), jnp.float32), 0.25, 1.75)
    expert_ids_keys = jax.random.split(jax.random.fold_in(seeds[9], 1), TOKENS // TOK_DEV)
    expert_ids_turns = jax.random.permutation(jax.random.fold_in(seeds[9], 3), TOKENS // TOK_DEV)
    expert_ids = jax.vmap(lambda own, number: routed_block(jax.random.fold_in(seeds[9], 2), own, number, TOK_DEV, EXPERTS, TOP, CAP, 2))(expert_ids_keys, expert_ids_turns).reshape((TOKENS, TOP))
    gate_values = jnp.clip(jnp.exp(math.log(1.0) - 2.3025851 * jax.random.uniform(seeds[10], (TOKENS, TOP), jnp.float32) ** levels(seeds[10], (TOKENS, TOP), ((0, 128),), -0.2, 0.2)), 0.1, 1.0)
    w_gate = normal_values(seeds[11], (2 * EXPERTS, D, FFW // 2), D ** -0.5, 0.0625, ((0, 64), (2, 2)))
    w_up = normal_values(seeds[12], (2 * EXPERTS, D, FFW // 2), D ** -0.5, 0.0625, ((0, 64), (2, 2)))
    w_down = normal_values(seeds[13], (2 * EXPERTS, FFW // 2, D), FFW ** -0.5, 0.1875, ((0, 64), (1, 2)))
    return {"query_latent": query_latent, "query_rope": query_rope, "cache_latent": cache_latent, "cache_rope": cache_rope, "lengths": lengths, "value_up": value_up, "out_proj": out_proj, "residual": residual, "norm_gain": norm_gain, "expert_ids": expert_ids, "gate_values": gate_values, "w_gate": w_gate, "w_up": w_up, "w_down": w_down}


softmax_scale = 192.0 ** (-0.5)

def attend_one(inputs):
    query_one, rope_one, cache_one, keys_one, length = inputs
    scores = jnp.dot(query_one, cache_one.T, preferred_element_type=jnp.float32)
    scores = scores + jnp.dot(rope_one, keys_one, preferred_element_type=jnp.float32)
    scores = scores * softmax_scale
    visible = jnp.arange(CTX, dtype=jnp.int32)[None, :] < length
    scores = jnp.where(visible, scores, -jnp.inf)
    row_peak = lax.optimization_barrier(jnp.max(scores, axis=1, keepdims=True))
    weights = jnp.exp(scores - row_peak)
    attn_weights = (weights / lax.optimization_barrier(jnp.sum(weights, axis=1, keepdims=True))).astype(jnp.bfloat16)
    return jnp.dot(attn_weights, cache_one, preferred_element_type=jnp.float32).astype(jnp.bfloat16)

def reference(query_latent, query_rope, cache_latent, cache_rope, lengths, value_up, out_proj, residual, norm_gain, expert_ids, gate_values, w_gate, w_up, w_down):
    mixed_latent = lax.map(attend_one, (query_latent, query_rope, cache_latent, cache_rope, lengths))
    head_values = jnp.einsum('thl,hlv->thv', mixed_latent.astype(jnp.float32), value_up.astype(jnp.float32)).astype(jnp.bfloat16)
    attention = jnp.dot(head_values.reshape(TOKENS, HEADS * VHEAD), out_proj, preferred_element_type=jnp.float32)
    stream = residual.astype(jnp.float32) + attention
    normed = (stream * lax.rsqrt(lax.optimization_barrier(jnp.mean(stream * stream, axis=1, keepdims=True)) + 1e-06) * norm_gain).astype(jnp.bfloat16)
    capacity = N_GROUP * N_DEV * CAP
    flat_ids = expert_ids.reshape(-1)
    flat_gates = gate_values.reshape(-1)
    token_of = (jnp.arange(TOKENS * TOP, dtype=jnp.int32) // TOP).astype(jnp.int32)

    def one_expert(running, expert):
        chosen = flat_ids == expert
        rank_of = jnp.cumsum(chosen.astype(jnp.int32)) - 1
        target = jnp.where(chosen, rank_of, capacity).astype(jnp.int32)
        row_ids = jnp.zeros((capacity + 1,), jnp.int32).at[target].set(token_of)[:capacity]
        slot_gates = jnp.zeros((capacity + 1,), jnp.float32).at[target].set(jnp.where(chosen, flat_gates, 0.0))[:capacity]
        picked = normed[row_ids]
        first_piece = expert * 2
        gate_w = jnp.concatenate([w_gate[first_piece], w_gate[first_piece + 1]], axis=1)
        up_w = jnp.concatenate([w_up[first_piece], w_up[first_piece + 1]], axis=1)
        down_w = jnp.concatenate([w_down[first_piece], w_down[first_piece + 1]], axis=0)
        gate_part = jnp.dot(picked, gate_w, preferred_element_type=jnp.float32)
        up_part = jnp.dot(picked, up_w, preferred_element_type=jnp.float32)
        active = (jax.nn.silu(gate_part) * up_part).astype(jnp.bfloat16)
        expert_out = jnp.dot(active, down_w, preferred_element_type=jnp.float32)
        running = running.at[row_ids].add(expert_out * slot_gates[:, None])
        return (running, None)
    mixture, _ = lax.scan(one_expert, jnp.zeros((TOKENS, D), jnp.float32), jnp.arange(EXPERTS, dtype=jnp.int32))
    return (stream + mixture).astype(jnp.bfloat16)
```

```python
import jax
import jax.numpy as jnp
from jax import lax
from jax.sharding import Mesh
from jax.sharding import PartitionSpec as P

DEV = ("dev_0", "dev_1", "dev_2", "dev_3")
GROUP_DEV = ("group", "dev_0", "dev_1", "dev_2", "dev_3")


softmax_scale = 192.0 ** (-0.5)


def attend(query_latent, query_rope, cache_latent, cache_rope, lengths):
    scores = jnp.einsum(
        "thl,tcl->thc", query_latent, cache_latent, preferred_element_type=jnp.float32
    )
    scores = scores + jnp.einsum(
        "thr,trc->thc", query_rope, cache_rope, preferred_element_type=jnp.float32
    )
    scores = scores * softmax_scale
    positions = lax.broadcasted_iota(jnp.int32, scores.shape, 2)
    scores = jnp.where(positions < lengths[:, None, None], scores, -jnp.inf)
    row_peak = jnp.max(scores, axis=2, keepdims=True)
    weights = jnp.exp(scores - row_peak)
    attn_weights = (weights / jnp.sum(weights, axis=2, keepdims=True)).astype(jnp.bfloat16)
    return jnp.einsum(
        "thc,tcl->thl", attn_weights, cache_latent, preferred_element_type=jnp.float32
    ).astype(jnp.bfloat16)


def expert_rows(token_rows, w_gate, w_up, w_down):
    gate_part = jnp.dot(token_rows, w_gate[0], preferred_element_type=jnp.float32)
    up_part = jnp.dot(token_rows, w_up[0], preferred_element_type=jnp.float32)
    active = (jax.nn.silu(gate_part) * up_part).astype(jnp.bfloat16)
    return jnp.dot(active, w_down[0], preferred_element_type=jnp.float32)


def local(
    query_latent,
    query_rope,
    cache_latent,
    cache_rope,
    lengths,
    value_up,
    out_proj,
    residual,
    norm_gain,
    expert_ids,
    gate_values,
    w_gate,
    w_up,
    w_down,
):
    tok_rows = query_latent.shape[0]
    feature_width = residual.shape[1]
    mixed_latent = attend(query_latent, query_rope, cache_latent, cache_rope, lengths)
    by_head = lax.all_to_all(mixed_latent, DEV, split_axis=1, concat_axis=0, tiled=True)
    head_values = jnp.einsum(
        "thl,hlv->thv", by_head, value_up, preferred_element_type=jnp.float32
    ).astype(jnp.bfloat16)
    flat_values = head_values.reshape(head_values.shape[0], -1)
    attention_part = jnp.dot(flat_values, out_proj, preferred_element_type=jnp.float32)
    attention = lax.psum_scatter(
        attention_part.astype(jnp.bfloat16), DEV, scatter_dimension=0, tiled=True
    ).astype(jnp.float32)
    stream = residual.astype(jnp.float32) + attention
    normed = (
        stream * lax.rsqrt(jnp.mean(stream * stream, axis=1, keepdims=True) + 1e-06) * norm_gain
    ).astype(jnp.bfloat16)
    experts = lax.axis_size(DEV) // 2
    expert_range = jnp.arange(experts, dtype=jnp.int32)
    chosen = expert_ids[:, :, None] == expert_range[None, None, :]
    row_gates = jnp.sum(jnp.where(chosen, gate_values[:, :, None], 0.0), axis=1)
    all_rows = lax.all_gather(normed, GROUP_DEV, axis=0, tiled=True)
    all_gates = lax.all_gather(row_gates, GROUP_DEV, axis=0, tiled=True)
    mine = lax.axis_index(DEV) // 2
    my_gates = jnp.sum(jnp.where(expert_range[None, :] == mine, all_gates, 0.0), axis=1)
    partial_value = expert_rows(all_rows, w_gate, w_up, w_down) * my_gates[:, None]
    mixture = lax.psum_scatter(
        partial_value.astype(jnp.bfloat16), GROUP_DEV, scatter_dimension=0, tiled=True
    ).astype(jnp.float32)
    return (stream + mixture).astype(jnp.bfloat16)


def solution(mesh):
    finer = Mesh(
        mesh.devices.reshape(mesh.shape["group"], 4, 2, 4, 2),
        ("group", "dev_0", "dev_1", "dev_2", "dev_3"),
    )
    return jax.shard_map(
        local,
        mesh=finer,
        in_specs=(
            P(GROUP_DEV, None, None),
            P(GROUP_DEV, None, None),
            P(GROUP_DEV, None, None),
            P(GROUP_DEV, None, None),
            P(GROUP_DEV),
            P(DEV, None, None),
            P(DEV, None),
            P(GROUP_DEV, None),
            P(),
            P(GROUP_DEV, None),
            P(GROUP_DEV, None),
            P(DEV, None, "group"),
            P(DEV, None, "group"),
            P(DEV, "group", None),
        ),
        out_specs=P(GROUP_DEV, None),
        check_vma=False,
    )
```

```python
import functools

import jax
import jax.numpy as jnp
from jax import lax
from jax.experimental import pallas as pl
from jax.experimental.pallas import tpu as pltpu
from jax.sharding import Mesh
from jax.sharding import PartitionSpec as P

DEV = ("dev_0", "dev_1", "dev_2", "dev_3")
GROUP_DEV = ("group", "dev_0", "dev_1", "dev_2", "dev_3")
MESH = pl.DeviceIdType.MESH


softmax_scale = 192.0 ** (-0.5)


def attend(query_latent, query_rope, cache_latent, cache_rope, lengths):
    scores = jnp.einsum(
        "thl,tcl->thc", query_latent, cache_latent, preferred_element_type=jnp.float32
    )
    scores = scores + jnp.einsum(
        "thr,trc->thc", query_rope, cache_rope, preferred_element_type=jnp.float32
    )
    scores = scores * softmax_scale
    positions = lax.broadcasted_iota(jnp.int32, scores.shape, 2)
    scores = jnp.where(positions < lengths[:, None, None], scores, -jnp.inf)
    row_peak = jnp.max(scores, axis=2, keepdims=True)
    weights = jnp.exp(scores - row_peak)
    attn_weights = (weights / jnp.sum(weights, axis=2, keepdims=True)).astype(jnp.bfloat16)
    return jnp.einsum(
        "thc,tcl->thl", attn_weights, cache_latent, preferred_element_type=jnp.float32
    ).astype(jnp.bfloat16)


HALF = 3584
UNIT = 256
ATTN_COLS = (((0, 1024), (1024, 768)), ((1792, 1024), (2816, 768)))
ATTN_ORDERS = (("z", "y"), ("y", "z"))
GATHER_COLS = (((0, 640), (640, 640)), ((1280, 640), (1920, 640)), ((2560, 640), (3200, 512)))
MIX_COLS = (((0, 768), (768, 512)), ((1280, 768), (2048, 512)), ((2560, 512), (3072, 512)))
ORDERS = (("z", "y", "x"), ("y", "x", "z"), ("x", "z", "y"))


def tail_kernel(
    values_ref,
    residual_ref,
    gain_ref,
    gates_ref,
    proj_hbm,
    gate_hbm,
    up_hbm,
    down_hbm,
    out_ref,
    proj,
    w_gate,
    w_up,
    w_down,
    attn_out,
    attn_in,
    attn_sum,
    attn_land0a,
    attn_land0b,
    attn_land1,
    attn_land2,
    attn_own,
    swap_out,
    swap_in,
    row_out,
    row_in,
    rows,
    gate_acc,
    up_acc,
    active,
    mix_out,
    mix_in,
    mix_sum,
    mix_land0,
    mix_land1,
    mix_land2,
    load_sem,
    send_sem,
    recv_sem,
):
    group = lax.axis_index("group")
    x_lo = lax.axis_index("dev_1")
    core = lax.axis_index("dev_3")
    pos = {"z": lax.axis_index("dev_0"), "y": lax.axis_index("dev_2"), "x": 2 * group + x_lo}
    other = 1 - core
    first_core = core == 0

    def above(dim):
        return lax.rem(pos[dim] + 1, 4)

    def below(dim):
        return lax.rem(pos[dim] + 3, 4)

    def across(dim):
        return lax.rem(pos[dim] + 2, 4)

    def device(dim, place):
        if dim == "z":
            return {"dev_0": place}
        if dim == "y":
            return {"dev_2": place}
        return {"group": lax.div(place, 2), "dev_1": lax.rem(place, 2)}

    partner = {"dev_3": other}
    x_pair = {"dev_1": 1 - x_lo}
    sent = []

    def send(src, dst, to):
        number = len(sent)
        copy = pltpu.make_async_remote_copy(
            src_ref=src,
            dst_ref=dst,
            send_sem=send_sem.at[number],
            recv_sem=recv_sem.at[number],
            device_id=to,
            device_id_type=MESH,
        )
        copy.start()
        sent.append(copy)
        return copy

    loads = []
    for number, (src, dst) in enumerate(
        ((proj_hbm, proj), (gate_hbm, w_gate), (up_hbm, w_up), (down_hbm, w_down))
    ):
        load = pltpu.make_async_copy(src, dst, load_sem.at[number])
        load.start()
        loads.append(load)

    barrier = pltpu.get_barrier_semaphore()
    pl.semaphore_signal(barrier, inc=1, device_id=partner, device_id_type=MESH)
    for dim in ("x", "y", "z"):
        for place in (above(dim), below(dim)):
            pl.semaphore_signal(barrier, inc=1, device_id=device(dim, place), device_id_type=MESH)
    pl.semaphore_wait(barrier, 7)

    def ring_start(dim, block, land, cols, part):
        first, second = cols
        up, down = device(dim, above(dim)), device(dim, below(dim))
        if part == 0:
            return (
                send(block(across(dim), first), land(0, first), up),
                send(block(below(dim), first), land(1, first), down),
            )
        return (
            send(block(across(dim), second), land(2, second), down),
            send(block(above(dim), second), land(3, second), up),
        )

    def add_into(target, *terms):
        total = target[...].astype(jnp.float32)
        for term in terms:
            total = total + term[...].astype(jnp.float32)
        return total

    def ring_relay(dim, block, land, cols, started):
        first, second = cols
        up, down = device(dim, above(dim)), device(dim, below(dim))
        started[0][0].wait_recv()
        target = block(above(dim), first)
        target[...] = add_into(target, land(0, first)).astype(jnp.bfloat16)
        upward = send(target, land(4, first), up)
        started[1][0].wait_recv()
        target = block(below(dim), second)
        target[...] = add_into(target, land(2, second)).astype(jnp.bfloat16)
        downward = send(target, land(5, second), down)
        return upward, downward

    def ring_finish(dim, block, land, cols, started, relayed, store):
        first, second = cols
        started[0][1].wait_recv()
        relayed[0].wait_recv()
        store(first, add_into(block(pos[dim], first), land(1, first), land(4, first)))
        started[1][1].wait_recv()
        relayed[1].wait_recv()
        store(second, add_into(block(pos[dim], second), land(3, second), land(5, second)))

    def span(cols):
        return pl.ds(cols[0], cols[1])

    def swap_halves(own):
        top, bottom = own[0:4, :], own[4:8, :]
        swap_out[...] = jnp.where(first_core, bottom, top)
        swapped = send(swap_out, swap_in.at[swap_count[0]], partner)
        swap_count[0] += 1
        swapped.wait_recv()
        mine = jnp.where(first_core, top, bottom)
        theirs = swap_in[swap_count[0] - 1]
        return jnp.where(first_core, mine, theirs), jnp.where(first_core, theirs, mine), swapped

    swap_count = [0]

    values = values_ref[...].reshape(256, 256)
    loads[0].wait()
    handed = {}

    def attn_units(cols, half, store):
        for start in range(cols[0], cols[0] + cols[1], UNIT):
            at = pl.multiple_of(half * HALF + start, 128)
            part = jnp.dot(
                values, proj[:, pl.ds(at, UNIT)], preferred_element_type=jnp.float32
            ).reshape(4, 2, 4, 8, UNIT)
            store(start, part)

    for rotation in range(2):
        for part in range(2):
            cols = ATTN_COLS[rotation][part]

            def store_out(start, value):
                attn_out[:, :, :, :, pl.ds(start, UNIT)] = value.astype(jnp.bfloat16)

            attn_units(cols, other, store_out)
            piece = (slice(None), slice(None), slice(None), slice(None), span(cols))
            handed[rotation, part] = send(attn_out.at[piece], attn_in.at[piece], partner)

    def attn_block(rotation, phase):
        dims = ATTN_ORDERS[rotation]

        def block(place, cols):
            at = {}
            for earlier in dims[:phase]:
                at[earlier] = pos[earlier]
            at[dims[phase]] = place
            return attn_sum.at[
                at.get("z", slice(None)), slice(None), at.get("y", slice(None)), slice(None), span(cols)
            ]

        return block

    def attn_land(rotation, phase):
        if phase == 0:
            land = (attn_land0a, attn_land0b)[rotation]
            return lambda slot, cols: land.at[
                slot, slice(None), slice(None), slice(None), pl.ds(0, cols[1])
            ]
        return lambda slot, cols: attn_land1.at[
            rotation, slot, slice(None), slice(None), pl.ds(0, cols[1])
        ]

    started = {}
    for rotation in range(2):
        dim = ATTN_ORDERS[rotation][0]
        for part in range(2):
            cols = ATTN_COLS[rotation][part]
            handed[rotation, part].wait_recv()

            def store_sum(start, value):
                at = (slice(None), slice(None), slice(None), slice(None), pl.ds(start, UNIT))
                total = value + attn_in[at].astype(jnp.float32)
                attn_sum[at] = total.astype(jnp.bfloat16)

            attn_units(cols, core, store_sum)
            started[rotation, part] = ring_start(
                dim, attn_block(rotation, 0), attn_land(rotation, 0), ATTN_COLS[rotation], part
            )
    paired = {}
    for phase in range(2):
        relayed = {}
        for rotation in range(2):
            relayed[rotation] = ring_relay(
                ATTN_ORDERS[rotation][phase],
                attn_block(rotation, phase),
                attn_land(rotation, phase),
                ATTN_COLS[rotation],
                (started[rotation, 0], started[rotation, 1]),
            )
        for rotation in range(2):
            dim = ATTN_ORDERS[rotation][phase]
            block = attn_block(rotation, phase)

            def store(cols, total):
                block(pos[dim], cols)[...] = total.astype(jnp.bfloat16)

            ring_finish(
                dim,
                block,
                attn_land(rotation, phase),
                ATTN_COLS[rotation],
                (started[rotation, 0], started[rotation, 1]),
                relayed[rotation],
                store,
            )
            if phase == 0:
                for part in range(2):
                    started[rotation, part] = ring_start(
                        ATTN_ORDERS[rotation][1],
                        attn_block(rotation, 1),
                        attn_land(rotation, 1),
                        ATTN_COLS[rotation],
                        part,
                    )
            else:
                width = ATTN_COLS[rotation][0][1] + ATTN_COLS[rotation][1][1]
                piece = pl.ds(ATTN_COLS[rotation][0][0], width)
                paired[rotation] = send(
                    attn_sum.at[pos["z"], 1 - x_lo, pos["y"], slice(None), piece],
                    attn_land2.at[slice(None), piece],
                    x_pair,
                )
    for rotation in range(2):
        paired[rotation].wait_recv()
    attn_own[...] = attn_sum[pos["z"], x_lo, pos["y"]].astype(jnp.float32) + attn_land2[
        ...
    ].astype(jnp.float32)
    low, high, swapped = swap_halves(attn_own)
    stream_low = residual_ref[:, 0:HALF].astype(jnp.float32) + low
    stream_high = residual_ref[:, HALF : 2 * HALF].astype(jnp.float32) + high
    square = jnp.sum(stream_low * stream_low, axis=1, keepdims=True) + jnp.sum(
        stream_high * stream_high, axis=1, keepdims=True
    )
    scale = lax.rsqrt(square / (2 * HALF) + 1e-06)
    dense = gates_ref[...]
    coarse = dense.astype(jnp.bfloat16).astype(jnp.float32)
    lane = lax.broadcasted_iota(jnp.int32, dense.shape, 1)
    packed = jnp.where(lane < 32, coarse, jnp.where(lane < 64, dense - coarse, 0.0))
    row_out[0, :, 0:HALF] = (stream_low * scale * gain_ref[:, 0:HALF]).astype(jnp.bfloat16)
    row_out[1, :, 0:HALF] = (stream_high * scale * gain_ref[:, HALF : 2 * HALF]).astype(
        jnp.bfloat16
    )
    row_out[0, :, HALF : HALF + 128] = packed.astype(jnp.bfloat16)
    row_out[1, :, HALF : HALF + 128] = packed.astype(jnp.bfloat16)
    handed_rows = send(row_out.at[other], row_in, partner)
    out_ref[:, 0:HALF] = stream_low
    out_ref[:, HALF : 2 * HALF] = stream_high

    handed_rows.wait_recv()
    mine = row_out[core].astype(jnp.float32)
    theirs = row_in[...].astype(jnp.float32)
    rows[core, pos["x"], pos["y"], pos["z"]] = jnp.concatenate(
        [jnp.where(first_core, mine, theirs), jnp.where(first_core, theirs, mine)], axis=0
    ).astype(jnp.bfloat16)

    def row_block(at, cols):
        return rows.at[
            core,
            at.get("x", slice(None)),
            at.get("y", slice(None)),
            at.get("z", slice(None)),
            slice(None),
            span(cols),
        ]

    shared = []
    for phase in range(3):
        opened = {}
        for rotation in range(3):
            dims = ORDERS[rotation]
            dim = dims[phase]
            first, second = GATHER_COLS[rotation]
            fixed = {later: pos[later] for later in dims[phase:]}
            up, down = device(dim, above(dim)), device(dim, below(dim))
            one, two = row_block(fixed, first), row_block(fixed, second)
            opened[rotation] = (
                send(one, one, up),
                send(two, two, down),
                send(two, two, up),
                send(one, one, down),
            )
            if phase == 2:
                whole = row_block(fixed, (first[0], first[1] + second[1]))
                shared.append(send(whole, whole, partner))
        forwarded = {}
        for rotation in range(3):
            dims = ORDERS[rotation]
            dim = dims[phase]
            first, second = GATHER_COLS[rotation]
            fixed = {later: pos[later] for later in dims[phase:]}
            up, down = device(dim, above(dim)), device(dim, below(dim))
            opened[rotation][0].wait_recv()
            one = row_block({**fixed, dim: below(dim)}, first)
            opened[rotation][1].wait_recv()
            two = row_block({**fixed, dim: above(dim)}, second)
            forwarded[rotation] = (send(one, one, up), send(two, two, down))
        for rotation in range(3):
            dims = ORDERS[rotation]
            dim = dims[phase]
            first, second = GATHER_COLS[rotation]
            fixed = {later: pos[later] for later in dims[phase:]}
            opened[rotation][2].wait_recv()
            opened[rotation][3].wait_recv()
            if phase == 2:
                for place in (below(dim), above(dim)):
                    whole = row_block({**fixed, dim: place}, (first[0], first[1] + second[1]))
                    shared.append(send(whole, whole, partner))
        for rotation in range(3):
            dims = ORDERS[rotation]
            dim = dims[phase]
            first, second = GATHER_COLS[rotation]
            fixed = {later: pos[later] for later in dims[phase:]}
            forwarded[rotation][0].wait_recv()
            forwarded[rotation][1].wait_recv()
            if phase == 2:
                whole = row_block({**fixed, dim: across(dim)}, (first[0], first[1] + second[1]))
                shared.append(send(whole, whole, partner))
    for copy in shared:
        copy.wait_recv()

    loads[1].wait()
    loads[2].wait()
    gate_acc[...] = jnp.zeros_like(gate_acc)
    up_acc[...] = jnp.zeros_like(up_acc)
    depth = 512
    for half in range(2):

        def product(step, carry):
            at = pl.multiple_of(step * depth, depth)
            row = pl.multiple_of(half * HALF + step * depth, depth)
            lhs = rows[half, :, :, :, :, pl.ds(at, depth)].reshape(512, depth)
            gate_acc[...] += jnp.dot(
                lhs, w_gate[pl.ds(row, depth), :], preferred_element_type=jnp.float32
            )
            up_acc[...] += jnp.dot(
                lhs, w_up[pl.ds(row, depth), :], preferred_element_type=jnp.float32
            )
            return carry

        lax.fori_loop(0, HALF // depth, product, 0)
    expert = (pos["z"] * 2 + x_lo) * 4 + pos["y"]
    parts = rows[0, :, :, :, :, HALF : HALF + 128].astype(jnp.float32).reshape(512, 128)
    lane = lax.broadcasted_iota(jnp.int32, parts.shape, 1)
    picked = jnp.where((lane == expert) | (lane == expert + 32), parts, 0.0)
    row_gate = jnp.sum(picked, axis=1, keepdims=True)
    gate_part = gate_acc[...]
    active[...] = (gate_part * jax.nn.sigmoid(gate_part) * up_acc[...] * row_gate).astype(
        jnp.bfloat16
    )

    loads[3].wait()

    def mix_units(cols, half, store):
        for start in range(cols[0], cols[0] + cols[1], UNIT):
            at = pl.multiple_of(half * HALF + start, 128)
            part = jnp.dot(
                active[...], w_down[:, pl.ds(at, UNIT)], preferred_element_type=jnp.float32
            ).reshape(4, 4, 4, 8, UNIT)
            store(start, part)

    for rotation in range(3):
        for part in range(2):
            cols = MIX_COLS[rotation][part]

            def store_out(start, value):
                mix_out[:, :, :, :, pl.ds(start, UNIT)] = value.astype(jnp.bfloat16)

            mix_units(cols, other, store_out)
            piece = (slice(None), slice(None), slice(None), slice(None), span(cols))
            handed[rotation, part] = send(mix_out.at[piece], mix_in.at[piece], partner)

    def mix_block(rotation, phase):
        dims = ORDERS[rotation][::-1]

        def block(place, cols):
            at = {}
            for earlier in dims[:phase]:
                at[earlier] = pos[earlier]
            at[dims[phase]] = place
            return mix_sum.at[
                at.get("x", slice(None)),
                at.get("y", slice(None)),
                at.get("z", slice(None)),
                slice(None),
                span(cols),
            ]

        return block

    def mix_land(rotation, phase):
        land = (mix_land0, mix_land1, mix_land2)[phase]

        def place(slot, cols):
            return land.at[
                (rotation, slot) + (slice(None),) * (3 - phase) + (pl.ds(0, cols[1]),)
            ]

        return place

    started = {}
    for rotation in range(3):
        for part in range(2):
            cols = MIX_COLS[rotation][part]
            handed[rotation, part].wait_recv()

            def store_sum(start, value):
                at = (slice(None), slice(None), slice(None), slice(None), pl.ds(start, UNIT))
                total = value + mix_in[at].astype(jnp.float32)
                mix_sum[at] = total.astype(jnp.bfloat16)

            mix_units(cols, core, store_sum)
            started[rotation, part] = ring_start(
                ORDERS[rotation][2], mix_block(rotation, 0), mix_land(rotation, 0), MIX_COLS[rotation], part
            )
    for phase in range(3):
        relayed = {}
        for rotation in range(3):
            relayed[rotation] = ring_relay(
                ORDERS[rotation][2 - phase],
                mix_block(rotation, phase),
                mix_land(rotation, phase),
                MIX_COLS[rotation],
                (started[rotation, 0], started[rotation, 1]),
            )
        for rotation in range(3):
            dim = ORDERS[rotation][2 - phase]
            block = mix_block(rotation, phase)

            def store(cols, total):
                if phase == 2:
                    attn_own[:, span(cols)] = total
                else:
                    block(pos[dim], cols)[...] = total.astype(jnp.bfloat16)

            ring_finish(
                dim,
                block,
                mix_land(rotation, phase),
                MIX_COLS[rotation],
                (started[rotation, 0], started[rotation, 1]),
                relayed[rotation],
                store,
            )
            if phase < 2:
                for part in range(2):
                    started[rotation, part] = ring_start(
                        ORDERS[rotation][1 - phase],
                        mix_block(rotation, phase + 1),
                        mix_land(rotation, phase + 1),
                        MIX_COLS[rotation],
                        part,
                    )
    swapped.wait_send()
    low, high, _ = swap_halves(attn_own)
    out_ref[:, 0:HALF] += low
    out_ref[:, HALF : 2 * HALF] += high
    for copy in sent:
        if copy is not swapped:
            copy.wait_send()


def layer_tail(values, residual, norm_gain, row_gates, out_proj, w_gate, w_up, w_down):
    bf16, f32 = jnp.bfloat16, jnp.float32
    vmem = pl.BlockSpec(memory_space=pltpu.VMEM)
    hbm = pl.BlockSpec(memory_space=pl.ANY)
    return pl.pallas_call(
        tail_kernel,
        out_shape=jax.ShapeDtypeStruct((4, 2 * HALF), f32),
        in_specs=[vmem] * 4 + [hbm] * 4,
        out_specs=vmem,
        scratch_shapes=[
            pltpu.VMEM(out_proj.shape, bf16),
            pltpu.VMEM(w_gate.shape, bf16),
            pltpu.VMEM(w_up.shape, bf16),
            pltpu.VMEM(w_down.shape, bf16),
            pltpu.VMEM((4, 2, 4, 8, HALF), bf16),
            pltpu.VMEM((4, 2, 4, 8, HALF), bf16),
            pltpu.VMEM((4, 2, 4, 8, HALF), bf16),
            pltpu.VMEM((6, 2, 4, 8, 1024), bf16),
            pltpu.VMEM((6, 4, 2, 8, 1024), bf16),
            pltpu.VMEM((2, 6, 2, 8, 1024), bf16),
            pltpu.VMEM((8, HALF), bf16),
            pltpu.VMEM((8, HALF), f32),
            pltpu.VMEM((4, HALF), f32),
            pltpu.VMEM((2, 4, HALF), f32),
            pltpu.VMEM((2, 4, HALF + 128), bf16),
            pltpu.VMEM((4, HALF + 128), bf16),
            pltpu.VMEM((2, 4, 4, 4, 8, HALF + 128), bf16),
            pltpu.VMEM((512, 256), f32),
            pltpu.VMEM((512, 256), f32),
            pltpu.VMEM((512, 256), bf16),
            pltpu.VMEM((4, 4, 4, 8, HALF), bf16),
            pltpu.VMEM((4, 4, 4, 8, HALF), bf16),
            pltpu.VMEM((4, 4, 4, 8, HALF), bf16),
            pltpu.VMEM((3, 6, 4, 4, 8, 768), bf16),
            pltpu.VMEM((3, 6, 4, 8, 768), bf16),
            pltpu.VMEM((3, 6, 8, 768), bf16),
            pltpu.SemaphoreType.DMA((4,)),
            pltpu.SemaphoreType.DMA((170,)),
            pltpu.SemaphoreType.DMA((170,)),
        ],
        compiler_params=pltpu.CompilerParams(
            collective_id=0, has_side_effects=True, vmem_limit_bytes=63 * 1024 * 1024
        ),
    )(values, residual, norm_gain, row_gates, out_proj, w_gate, w_up, w_down).astype(bf16)


def local(
    query_latent,
    query_rope,
    cache_latent,
    cache_rope,
    lengths,
    value_up,
    out_proj,
    residual,
    norm_gain,
    expert_ids,
    gate_values,
    w_gate,
    w_up,
    w_down,
):
    mixed_latent = attend(query_latent, query_rope, cache_latent, cache_rope, lengths)
    by_head = lax.all_to_all(mixed_latent, DEV, split_axis=1, concat_axis=0, tiled=True)
    head_values = jnp.einsum(
        "thl,hlv->thv", by_head, value_up, preferred_element_type=jnp.float32
    ).astype(jnp.bfloat16)
    flat_values = head_values.reshape(4, 2, 4, 8, 256)
    experts = lax.axis_size(DEV) // 2
    expert_range = jnp.arange(128, dtype=jnp.int32) % experts
    chosen = expert_ids[:, :, None] == expert_range[None, None, :]
    row_gates = jnp.sum(jnp.where(chosen, gate_values[:, :, None], 0.0), axis=1)
    return layer_tail(
        flat_values,
        residual,
        norm_gain[None, :],
        row_gates,
        out_proj,
        w_gate[0],
        w_up[0],
        w_down[0],
    )


def solution(mesh):
    finer = Mesh(
        mesh.devices.reshape(mesh.shape["group"], 4, 2, 4, 2),
        ("group", "dev_0", "dev_1", "dev_2", "dev_3"),
    )
    return jax.shard_map(
        local,
        mesh=finer,
        in_specs=(
            P(GROUP_DEV, None, None),
            P(GROUP_DEV, None, None),
            P(GROUP_DEV, None, None),
            P(GROUP_DEV, None, None),
            P(GROUP_DEV),
            P(DEV, None, None),
            P(DEV, None),
            P(GROUP_DEV, None),
            P(),
            P(GROUP_DEV, None),
            P(GROUP_DEV, None),
            P(DEV, None, "group"),
            P(DEV, None, "group"),
            P(DEV, "group", None),
        ),
        out_specs=P(GROUP_DEV, None),
        check_vma=False,
    )
```

```python
import functools

import jax
import jax.numpy as jnp
from jax import lax
from jax.experimental import pallas as pl
from jax.experimental.pallas import tpu as pltpu
from jax.sharding import Mesh
from jax.sharding import PartitionSpec as P

DEV = ("dev_0", "dev_1", "dev_2", "dev_3")
GROUP_DEV = ("group", "dev_0", "dev_1", "dev_2", "dev_3")
MESH = pl.DeviceIdType.MESH


softmax_scale = 192.0 ** (-0.5)


HALF = 3584
UNIT = 256
ATTN_COLS = (((0, 1024), (1024, 768)), ((1792, 1024), (2816, 768)))
ATTN_ORDERS = (("z", "y"), ("y", "z"))
GATHER_COLS = (((0, 640), (640, 640)), ((1280, 640), (1920, 640)), ((2560, 640), (3200, 512)))
MIX_COLS = (((0, 768), (768, 512)), ((1280, 768), (2048, 512)), ((2560, 512), (3072, 512)))
ORDERS = (("z", "y", "x"), ("y", "x", "z"), ("x", "z", "y"))


def layer_kernel(
    lengths_ref,
    residual_ref,
    gain_ref,
    gates_ref,
    query_hbm,
    query_rope_hbm,
    cache_hbm,
    cache_rope_hbm,
    value_hbm,
    proj_hbm,
    gate_hbm,
    up_hbm,
    down_hbm,
    out_ref,
    query,
    query_rope,
    cache,
    cache_rope,
    scores,
    probs,
    latent_out,
    latent_in,
    value_up,
    even_part,
    odd_part,
    even_values,
    odd_values,
    proj,
    w_gate,
    w_up,
    w_down,
    attn_out,
    attn_in,
    attn_sum,
    attn_land0a,
    attn_land0b,
    attn_land1,
    attn_land2,
    attn_own,
    swap_out,
    swap_in,
    row_out,
    row_in,
    rows,
    gate_acc,
    up_acc,
    active,
    mix_out,
    mix_in,
    mix_sum,
    mix_land0,
    mix_land1,
    mix_land2,
    cache_sem,
    load_sem,
    latent_send,
    latent_recv,
    send_sem,
    recv_sem,
):
    group = lax.axis_index("group")
    x_lo = lax.axis_index("dev_1")
    core = lax.axis_index("dev_3")
    pos = {"z": lax.axis_index("dev_0"), "y": lax.axis_index("dev_2"), "x": 2 * group + x_lo}
    other = 1 - core
    first_core = core == 0

    def above(dim):
        return lax.rem(pos[dim] + 1, 4)

    def below(dim):
        return lax.rem(pos[dim] + 3, 4)

    def across(dim):
        return lax.rem(pos[dim] + 2, 4)

    def device(dim, place):
        if dim == "z":
            return {"dev_0": place}
        if dim == "y":
            return {"dev_2": place}
        return {"group": lax.div(place, 2), "dev_1": lax.rem(place, 2)}

    partner = {"dev_3": other}
    x_pair = {"dev_1": 1 - x_lo}
    sent = []

    def send(src, dst, to):
        number = len(sent)
        copy = pltpu.make_async_remote_copy(
            src_ref=src,
            dst_ref=dst,
            send_sem=send_sem.at[number],
            recv_sem=recv_sem.at[number],
            device_id=to,
            device_id_type=MESH,
        )
        copy.start()
        sent.append(copy)
        return copy

    def load(number, src, dst):
        copy = pltpu.make_async_copy(src, dst, load_sem.at[number])
        copy.start()
        return copy

    def load_cache(token):
        slot = token % 2
        copy = pltpu.make_async_copy(cache_hbm.at[token], cache.at[slot], cache_sem.at[slot])
        copy.start()
        return copy

    query_load = load(4, query_hbm, query)
    query_rope_load = load(5, query_rope_hbm, query_rope)
    cache_loads = [load_cache(0)]
    cache_rope_load = load(6, cache_rope_hbm, cache_rope)
    cache_loads.append(load_cache(1))

    place = ((pos["z"] * 2 + x_lo) * 4 + pos["y"]) * 2 + core

    def peer(step):
        number = lax.rem(place + step, 64)
        return number, {
            "dev_0": lax.div(number, 16),
            "dev_1": lax.rem(lax.div(number, 8), 2),
            "dev_2": lax.rem(lax.div(number, 2), 4),
            "dev_3": lax.rem(number, 2),
        }

    barrier = pltpu.get_barrier_semaphore()

    def greet(step, carry):
        pl.semaphore_signal(barrier, inc=1, device_id=peer(step)[1], device_id_type=MESH)
        return carry

    lax.fori_loop(1, 64, greet, 0)
    outer_x = lax.rem(pos["x"] + 3 + 2 * x_lo, 4)
    pl.semaphore_signal(barrier, inc=1, device_id=device("x", outer_x), device_id_type=MESH)

    query_load.wait()
    query_rope_load.wait()
    loads = {}
    for token in range(4):
        slot = token % 2
        cache_loads[token].wait()
        if token == 0:
            cache_rope_load.wait()
            loads["value"] = load(7, value_hbm, value_up)
            loads["proj"] = load(0, proj_hbm, proj)
        length = lengths_ref[token]
        peak = jnp.full((128, 1), -jnp.inf, jnp.float32)
        for start in range(0, 2048, 512):
            cols = pl.ds(start, 512)
            part = lax.dot_general(
                query[token],
                cache[slot, cols, :],
                (((1,), (1,)), ((), ())),
                preferred_element_type=jnp.float32,
            ) + lax.dot_general(
                query_rope[token],
                cache_rope[token, :, cols],
                (((0,), (0,)), ((), ())),
                preferred_element_type=jnp.float32,
            )
            slots = lax.broadcasted_iota(jnp.int32, part.shape, 1) + start
            part = jnp.where(slots < length, part, -jnp.inf)
            scores[:, cols] = part
            peak = jnp.maximum(peak, jnp.max(part, axis=1, keepdims=True))
        total = jnp.zeros((128, 1), jnp.float32)
        for start in range(0, 2048, 512):
            cols = pl.ds(start, 512)
            weights = jnp.exp((scores[:, cols] - peak) * softmax_scale)
            total = total + jnp.sum(weights, axis=1, keepdims=True)
            probs[:, cols] = weights.astype(jnp.bfloat16)
        mixed = jnp.dot(probs[...], cache[slot], preferred_element_type=jnp.float32) / total
        latent_out[token] = mixed.reshape(64, 2, 512).astype(jnp.bfloat16)
        if token + 2 < 4:
            cache_loads.append(load_cache(token + 2))
        if token == 0:
            pl.semaphore_wait(barrier, 64)
        elif token == 1:
            loads["gate"] = load(1, gate_hbm, w_gate)
        elif token == 2:
            loads["up"] = load(2, up_hbm, w_up)
            loads["down"] = load(3, down_hbm, w_down)

        def scatter(step, carry):
            number, to = peer(step)
            pltpu.make_async_remote_copy(
                src_ref=latent_out.at[token, number],
                dst_ref=latent_in.at[token, place],
                send_sem=latent_send.at[token],
                recv_sem=latent_recv.at[token],
                device_id=to,
                device_id_type=MESH,
            ).start()
            return carry

        lax.fori_loop(1, 64, scatter, 0)
        latent_in[token, place] = latent_out[token, place]

    def latent_copies(token):
        return pltpu.make_async_remote_copy(
            src_ref=latent_out.at[token, pl.ds(0, 63)],
            dst_ref=latent_in.at[token, pl.ds(0, 63)],
            send_sem=latent_send.at[token],
            recv_sem=latent_recv.at[token],
            device_id=partner,
            device_id_type=MESH,
        )

    loads["value"].wait()
    for token in range(4):
        latent_copies(token).wait_recv()
        latents = latent_in[token].reshape(128, 512)
        even_part[...] = jnp.dot(latents, value_up[0], preferred_element_type=jnp.float32)
        odd_part[...] = jnp.dot(latents, value_up[1], preferred_element_type=jnp.float32)
        even_values[pl.ds(token, 64, stride=4), :] = even_part[pl.ds(0, 64, stride=2), :]
        odd_values[pl.ds(token, 64, stride=4), :] = odd_part[pl.ds(1, 64, stride=2), :]
    values = jnp.concatenate([even_values[...], odd_values[...]], axis=1).astype(jnp.bfloat16)

    def ring_start(dim, block, land, cols, part):
        first, second = cols
        up, down = device(dim, above(dim)), device(dim, below(dim))
        if part == 0:
            return (
                send(block(across(dim), first), land(0, first), up),
                send(block(below(dim), first), land(1, first), down),
            )
        return (
            send(block(across(dim), second), land(2, second), down),
            send(block(above(dim), second), land(3, second), up),
        )

    def add_into(target, *terms):
        total = target[...].astype(jnp.float32)
        for term in terms:
            total = total + term[...].astype(jnp.float32)
        return total

    def ring_relay(dim, block, land, cols, started):
        first, second = cols
        up, down = device(dim, above(dim)), device(dim, below(dim))
        started[0][0].wait_recv()
        target = block(above(dim), first)
        target[...] = add_into(target, land(0, first)).astype(jnp.bfloat16)
        upward = send(target, land(4, first), up)
        started[1][0].wait_recv()
        target = block(below(dim), second)
        target[...] = add_into(target, land(2, second)).astype(jnp.bfloat16)
        downward = send(target, land(5, second), down)
        return upward, downward

    def ring_finish(dim, block, land, cols, started, relayed, store):
        first, second = cols
        started[0][1].wait_recv()
        relayed[0].wait_recv()
        store(first, add_into(block(pos[dim], first), land(1, first), land(4, first)))
        started[1][1].wait_recv()
        relayed[1].wait_recv()
        store(second, add_into(block(pos[dim], second), land(3, second), land(5, second)))

    def span(cols):
        return pl.ds(cols[0], cols[1])

    def swap_halves(own):
        top, bottom = own[0:4, :], own[4:8, :]
        swap_out[...] = jnp.where(first_core, bottom, top)
        swapped = send(swap_out, swap_in.at[swap_count[0]], partner)
        swap_count[0] += 1
        swapped.wait_recv()
        mine = jnp.where(first_core, top, bottom)
        theirs = swap_in[swap_count[0] - 1]
        return jnp.where(first_core, mine, theirs), jnp.where(first_core, theirs, mine), swapped

    swap_count = [0]

    loads["proj"].wait()
    handed = {}

    def attn_units(cols, half, store):
        for start in range(cols[0], cols[0] + cols[1], UNIT):
            at = pl.multiple_of(half * HALF + start, 128)
            part = jnp.dot(
                values, proj[:, pl.ds(at, UNIT)], preferred_element_type=jnp.float32
            ).reshape(4, 2, 4, 8, UNIT)
            store(start, part)

    for rotation in range(2):
        for part in range(2):
            cols = ATTN_COLS[rotation][part]

            def store_out(start, value):
                attn_out[:, :, :, :, pl.ds(start, UNIT)] = value.astype(jnp.bfloat16)

            attn_units(cols, other, store_out)
            piece = (slice(None), slice(None), slice(None), slice(None), span(cols))
            handed[rotation, part] = send(attn_out.at[piece], attn_in.at[piece], partner)

    def attn_block(rotation, phase):
        dims = ATTN_ORDERS[rotation]

        def block(place, cols):
            at = {}
            for earlier in dims[:phase]:
                at[earlier] = pos[earlier]
            at[dims[phase]] = place
            return attn_sum.at[
                at.get("z", slice(None)), slice(None), at.get("y", slice(None)), slice(None), span(cols)
            ]

        return block

    def attn_land(rotation, phase):
        if phase == 0:
            land = (attn_land0a, attn_land0b)[rotation]
            return lambda slot, cols: land.at[
                slot, slice(None), slice(None), slice(None), pl.ds(0, cols[1])
            ]
        return lambda slot, cols: attn_land1.at[
            rotation, slot, slice(None), slice(None), pl.ds(0, cols[1])
        ]

    started = {}
    for rotation in range(2):
        dim = ATTN_ORDERS[rotation][0]
        for part in range(2):
            cols = ATTN_COLS[rotation][part]
            handed[rotation, part].wait_recv()

            def store_sum(start, value):
                at = (slice(None), slice(None), slice(None), slice(None), pl.ds(start, UNIT))
                total = value + attn_in[at].astype(jnp.float32)
                attn_sum[at] = total.astype(jnp.bfloat16)

            attn_units(cols, core, store_sum)
            started[rotation, part] = ring_start(
                dim, attn_block(rotation, 0), attn_land(rotation, 0), ATTN_COLS[rotation], part
            )
    paired = {}
    for phase in range(2):
        relayed = {}
        for rotation in range(2):
            relayed[rotation] = ring_relay(
                ATTN_ORDERS[rotation][phase],
                attn_block(rotation, phase),
                attn_land(rotation, phase),
                ATTN_COLS[rotation],
                (started[rotation, 0], started[rotation, 1]),
            )
        for rotation in range(2):
            dim = ATTN_ORDERS[rotation][phase]
            block = attn_block(rotation, phase)

            def store(cols, total):
                block(pos[dim], cols)[...] = total.astype(jnp.bfloat16)

            ring_finish(
                dim,
                block,
                attn_land(rotation, phase),
                ATTN_COLS[rotation],
                (started[rotation, 0], started[rotation, 1]),
                relayed[rotation],
                store,
            )
            if phase == 0:
                for part in range(2):
                    started[rotation, part] = ring_start(
                        ATTN_ORDERS[rotation][1],
                        attn_block(rotation, 1),
                        attn_land(rotation, 1),
                        ATTN_COLS[rotation],
                        part,
                    )
            else:
                width = ATTN_COLS[rotation][0][1] + ATTN_COLS[rotation][1][1]
                piece = pl.ds(ATTN_COLS[rotation][0][0], width)
                paired[rotation] = send(
                    attn_sum.at[pos["z"], 1 - x_lo, pos["y"], slice(None), piece],
                    attn_land2.at[slice(None), piece],
                    x_pair,
                )
    for rotation in range(2):
        paired[rotation].wait_recv()
    attn_own[...] = attn_sum[pos["z"], x_lo, pos["y"]].astype(jnp.float32) + attn_land2[
        ...
    ].astype(jnp.float32)
    low, high, swapped = swap_halves(attn_own)
    stream_low = residual_ref[:, 0:HALF].astype(jnp.float32) + low
    stream_high = residual_ref[:, HALF : 2 * HALF].astype(jnp.float32) + high
    square = jnp.sum(stream_low * stream_low, axis=1, keepdims=True) + jnp.sum(
        stream_high * stream_high, axis=1, keepdims=True
    )
    scale = lax.rsqrt(square / (2 * HALF) + 1e-06)
    dense = gates_ref[...]
    coarse = dense.astype(jnp.bfloat16).astype(jnp.float32)
    lane = lax.broadcasted_iota(jnp.int32, dense.shape, 1)
    packed = jnp.where(lane < 32, coarse, jnp.where(lane < 64, dense - coarse, 0.0))
    row_out[0, :, 0:HALF] = (stream_low * scale * gain_ref[:, 0:HALF]).astype(jnp.bfloat16)
    row_out[1, :, 0:HALF] = (stream_high * scale * gain_ref[:, HALF : 2 * HALF]).astype(
        jnp.bfloat16
    )
    row_out[0, :, HALF : HALF + 128] = packed.astype(jnp.bfloat16)
    row_out[1, :, HALF : HALF + 128] = packed.astype(jnp.bfloat16)
    handed_rows = send(row_out.at[other], row_in, partner)
    out_ref[:, 0:HALF] = stream_low
    out_ref[:, HALF : 2 * HALF] = stream_high

    handed_rows.wait_recv()
    mine = row_out[core].astype(jnp.float32)
    theirs = row_in[...].astype(jnp.float32)
    rows[core, pos["x"], pos["y"], pos["z"]] = jnp.concatenate(
        [jnp.where(first_core, mine, theirs), jnp.where(first_core, theirs, mine)], axis=0
    ).astype(jnp.bfloat16)

    def row_block(at, cols):
        return rows.at[
            core,
            at.get("x", slice(None)),
            at.get("y", slice(None)),
            at.get("z", slice(None)),
            slice(None),
            span(cols),
        ]

    shared = []
    for phase in range(3):
        opened = {}
        for rotation in range(3):
            dims = ORDERS[rotation]
            dim = dims[phase]
            first, second = GATHER_COLS[rotation]
            fixed = {later: pos[later] for later in dims[phase:]}
            up, down = device(dim, above(dim)), device(dim, below(dim))
            one, two = row_block(fixed, first), row_block(fixed, second)
            opened[rotation] = (
                send(one, one, up),
                send(two, two, down),
                send(two, two, up),
                send(one, one, down),
            )
            if phase == 2:
                whole = row_block(fixed, (first[0], first[1] + second[1]))
                shared.append(send(whole, whole, partner))
        forwarded = {}
        for rotation in range(3):
            dims = ORDERS[rotation]
            dim = dims[phase]
            first, second = GATHER_COLS[rotation]
            fixed = {later: pos[later] for later in dims[phase:]}
            up, down = device(dim, above(dim)), device(dim, below(dim))
            opened[rotation][0].wait_recv()
            one = row_block({**fixed, dim: below(dim)}, first)
            opened[rotation][1].wait_recv()
            two = row_block({**fixed, dim: above(dim)}, second)
            forwarded[rotation] = (send(one, one, up), send(two, two, down))
        for rotation in range(3):
            dims = ORDERS[rotation]
            dim = dims[phase]
            first, second = GATHER_COLS[rotation]
            fixed = {later: pos[later] for later in dims[phase:]}
            opened[rotation][2].wait_recv()
            opened[rotation][3].wait_recv()
            if phase == 2:
                for place in (below(dim), above(dim)):
                    whole = row_block({**fixed, dim: place}, (first[0], first[1] + second[1]))
                    shared.append(send(whole, whole, partner))
        for rotation in range(3):
            dims = ORDERS[rotation]
            dim = dims[phase]
            first, second = GATHER_COLS[rotation]
            fixed = {later: pos[later] for later in dims[phase:]}
            forwarded[rotation][0].wait_recv()
            forwarded[rotation][1].wait_recv()
            if phase == 2:
                whole = row_block({**fixed, dim: across(dim)}, (first[0], first[1] + second[1]))
                shared.append(send(whole, whole, partner))
    for copy in shared:
        copy.wait_recv()

    loads["gate"].wait()
    loads["up"].wait()
    gate_acc[...] = jnp.zeros_like(gate_acc)
    up_acc[...] = jnp.zeros_like(up_acc)
    depth = 512
    for half in range(2):

        def product(step, carry):
            at = pl.multiple_of(step * depth, depth)
            row = pl.multiple_of(half * HALF + step * depth, depth)
            lhs = rows[half, :, :, :, :, pl.ds(at, depth)].reshape(512, depth)
            gate_acc[...] += jnp.dot(
                lhs, w_gate[pl.ds(row, depth), :], preferred_element_type=jnp.float32
            )
            up_acc[...] += jnp.dot(
                lhs, w_up[pl.ds(row, depth), :], preferred_element_type=jnp.float32
            )
            return carry

        lax.fori_loop(0, HALF // depth, product, 0)
    expert = (pos["z"] * 2 + x_lo) * 4 + pos["y"]
    parts = rows[0, :, :, :, :, HALF : HALF + 128].astype(jnp.float32).reshape(512, 128)
    lane = lax.broadcasted_iota(jnp.int32, parts.shape, 1)
    picked = jnp.where((lane == expert) | (lane == expert + 32), parts, 0.0)
    row_gate = jnp.sum(picked, axis=1, keepdims=True)
    gate_part = gate_acc[...]
    active[...] = (gate_part * jax.nn.sigmoid(gate_part) * up_acc[...] * row_gate).astype(
        jnp.bfloat16
    )

    loads["down"].wait()

    def mix_units(cols, half, store):
        for start in range(cols[0], cols[0] + cols[1], UNIT):
            at = pl.multiple_of(half * HALF + start, 128)
            part = jnp.dot(
                active[...], w_down[:, pl.ds(at, UNIT)], preferred_element_type=jnp.float32
            ).reshape(4, 4, 4, 8, UNIT)
            store(start, part)

    for rotation in range(3):
        for part in range(2):
            cols = MIX_COLS[rotation][part]

            def store_out(start, value):
                mix_out[:, :, :, :, pl.ds(start, UNIT)] = value.astype(jnp.bfloat16)

            mix_units(cols, other, store_out)
            piece = (slice(None), slice(None), slice(None), slice(None), span(cols))
            handed[rotation, part] = send(mix_out.at[piece], mix_in.at[piece], partner)

    def mix_block(rotation, phase):
        dims = ORDERS[rotation][::-1]

        def block(place, cols):
            at = {}
            for earlier in dims[:phase]:
                at[earlier] = pos[earlier]
            at[dims[phase]] = place
            return mix_sum.at[
                at.get("x", slice(None)),
                at.get("y", slice(None)),
                at.get("z", slice(None)),
                slice(None),
                span(cols),
            ]

        return block

    def mix_land(rotation, phase):
        land = (mix_land0, mix_land1, mix_land2)[phase]

        def place(slot, cols):
            return land.at[
                (rotation, slot) + (slice(None),) * (3 - phase) + (pl.ds(0, cols[1]),)
            ]

        return place

    started = {}
    for rotation in range(3):
        for part in range(2):
            cols = MIX_COLS[rotation][part]
            handed[rotation, part].wait_recv()

            def store_sum(start, value):
                at = (slice(None), slice(None), slice(None), slice(None), pl.ds(start, UNIT))
                total = value + mix_in[at].astype(jnp.float32)
                mix_sum[at] = total.astype(jnp.bfloat16)

            mix_units(cols, core, store_sum)
            started[rotation, part] = ring_start(
                ORDERS[rotation][2], mix_block(rotation, 0), mix_land(rotation, 0), MIX_COLS[rotation], part
            )
    for phase in range(3):
        relayed = {}
        for rotation in range(3):
            relayed[rotation] = ring_relay(
                ORDERS[rotation][2 - phase],
                mix_block(rotation, phase),
                mix_land(rotation, phase),
                MIX_COLS[rotation],
                (started[rotation, 0], started[rotation, 1]),
            )
        for rotation in range(3):
            dim = ORDERS[rotation][2 - phase]
            block = mix_block(rotation, phase)

            def store(cols, total):
                if phase == 2:
                    attn_own[:, span(cols)] = total
                else:
                    block(pos[dim], cols)[...] = total.astype(jnp.bfloat16)

            ring_finish(
                dim,
                block,
                mix_land(rotation, phase),
                MIX_COLS[rotation],
                (started[rotation, 0], started[rotation, 1]),
                relayed[rotation],
                store,
            )
            if phase < 2:
                for part in range(2):
                    started[rotation, part] = ring_start(
                        ORDERS[rotation][1 - phase],
                        mix_block(rotation, phase + 1),
                        mix_land(rotation, phase + 1),
                        MIX_COLS[rotation],
                        part,
                    )
    swapped.wait_send()
    low, high, _ = swap_halves(attn_own)
    out_ref[:, 0:HALF] += low
    out_ref[:, HALF : 2 * HALF] += high
    for copy in sent:
        if copy is not swapped:
            copy.wait_send()
    for token in range(4):
        latent_copies(token).wait_send()


def layer(
    lengths,
    residual,
    norm_gain,
    row_gates,
    query_latent,
    query_rope,
    cache_latent,
    cache_rope,
    value_up,
    out_proj,
    w_gate,
    w_up,
    w_down,
):
    bf16, f32 = jnp.bfloat16, jnp.float32
    vmem = pl.BlockSpec(memory_space=pltpu.VMEM)
    hbm = pl.BlockSpec(memory_space=pl.ANY)
    return pl.pallas_call(
        layer_kernel,
        out_shape=jax.ShapeDtypeStruct((4, 2 * HALF), f32),
        in_specs=[pl.BlockSpec(memory_space=pltpu.SMEM)] + [vmem] * 3 + [hbm] * 9,
        out_specs=vmem,
        scratch_shapes=[
            pltpu.VMEM(query_latent.shape, bf16),
            pltpu.VMEM(query_rope.shape, bf16),
            pltpu.VMEM((2, 2048, 512), bf16),
            pltpu.VMEM(cache_rope.shape, bf16),
            pltpu.VMEM((128, 2048), f32),
            pltpu.VMEM((128, 2048), bf16),
            pltpu.VMEM((4, 64, 2, 512), bf16),
            pltpu.VMEM((4, 64, 2, 512), bf16),
            pltpu.VMEM(value_up.shape, bf16),
            pltpu.VMEM((128, 128), f32),
            pltpu.VMEM((128, 128), f32),
            pltpu.VMEM((256, 128), f32),
            pltpu.VMEM((256, 128), f32),
            pltpu.VMEM(out_proj.shape, bf16),
            pltpu.VMEM(w_gate.shape, bf16),
            pltpu.VMEM(w_up.shape, bf16),
            pltpu.VMEM(w_down.shape, bf16),
            pltpu.VMEM((4, 2, 4, 8, HALF), bf16),
            pltpu.VMEM((4, 2, 4, 8, HALF), bf16),
            pltpu.VMEM((4, 2, 4, 8, HALF), bf16),
            pltpu.VMEM((6, 2, 4, 8, 1024), bf16),
            pltpu.VMEM((6, 4, 2, 8, 1024), bf16),
            pltpu.VMEM((2, 6, 2, 8, 1024), bf16),
            pltpu.VMEM((8, HALF), bf16),
            pltpu.VMEM((8, HALF), f32),
            pltpu.VMEM((4, HALF), f32),
            pltpu.VMEM((2, 4, HALF), f32),
            pltpu.VMEM((2, 4, HALF + 128), bf16),
            pltpu.VMEM((4, HALF + 128), bf16),
            pltpu.VMEM((2, 4, 4, 4, 8, HALF + 128), bf16),
            pltpu.VMEM((512, 256), f32),
            pltpu.VMEM((512, 256), f32),
            pltpu.VMEM((512, 256), bf16),
            pltpu.VMEM((4, 4, 4, 8, HALF), bf16),
            pltpu.VMEM((4, 4, 4, 8, HALF), bf16),
            pltpu.VMEM((4, 4, 4, 8, HALF), bf16),
            pltpu.VMEM((3, 6, 4, 4, 8, 768), bf16),
            pltpu.VMEM((3, 6, 4, 8, 768), bf16),
            pltpu.VMEM((3, 6, 8, 768), bf16),
            pltpu.SemaphoreType.DMA((2,)),
            pltpu.SemaphoreType.DMA((8,)),
            pltpu.SemaphoreType.DMA((4,)),
            pltpu.SemaphoreType.DMA((4,)),
            pltpu.SemaphoreType.DMA((170,)),
            pltpu.SemaphoreType.DMA((170,)),
        ],
        compiler_params=pltpu.CompilerParams(
            collective_id=0, has_side_effects=True, vmem_limit_bytes=63 * 1024 * 1024
        ),
    )(
        lengths,
        residual,
        norm_gain,
        row_gates,
        query_latent,
        query_rope,
        cache_latent,
        cache_rope,
        value_up,
        out_proj,
        w_gate,
        w_up,
        w_down,
    ).astype(bf16)


def local(
    query_latent,
    query_rope,
    cache_latent,
    cache_rope,
    lengths,
    value_up,
    out_proj,
    residual,
    norm_gain,
    expert_ids,
    gate_values,
    w_gate,
    w_up,
    w_down,
):
    experts = lax.axis_size(DEV) // 2
    expert_range = jnp.arange(128, dtype=jnp.int32) % experts
    chosen = expert_ids[:, :, None] == expert_range[None, None, :]
    row_gates = jnp.sum(jnp.where(chosen, gate_values[:, :, None], 0.0), axis=1)
    return layer(
        lengths,
        residual,
        norm_gain[None, :],
        row_gates,
        query_latent,
        jnp.swapaxes(query_rope, 1, 2),
        cache_latent,
        cache_rope,
        value_up,
        out_proj,
        w_gate[0],
        w_up[0],
        w_down[0],
    )


def solution(mesh):
    finer = Mesh(
        mesh.devices.reshape(mesh.shape["group"], 4, 2, 4, 2),
        ("group", "dev_0", "dev_1", "dev_2", "dev_3"),
    )
    return jax.shard_map(
        local,
        mesh=finer,
        in_specs=(
            P(GROUP_DEV, None, None),
            P(GROUP_DEV, None, None),
            P(GROUP_DEV, None, None),
            P(GROUP_DEV, None, None),
            P(GROUP_DEV),
            P(DEV, None, None),
            P(DEV, None),
            P(GROUP_DEV, None),
            P(),
            P(GROUP_DEV, None),
            P(GROUP_DEV, None),
            P(DEV, None, "group"),
            P(DEV, None, "group"),
            P(DEV, "group", None),
        ),
        out_specs=P(GROUP_DEV, None),
        check_vma=False,
    )
```

```python
import functools

import jax
import jax.numpy as jnp
from jax import lax
from jax.experimental import pallas as pl
from jax.experimental.pallas import tpu as pltpu
from jax.sharding import Mesh
from jax.sharding import PartitionSpec as P

DEV = ("dev_0", "dev_1", "dev_2", "dev_3")
GROUP_DEV = ("group", "dev_0", "dev_1", "dev_2", "dev_3")
MESH = pl.DeviceIdType.MESH


softmax_scale = 192.0 ** (-0.5)


HALF = 3584
UNIT = 256
ATTN_COLS = (((0, 1024), (1024, 768)), ((1792, 1024), (2816, 768)))
ATTN_ORDERS = (("z", "y"), ("y", "z"))
GATHER_COLS = (((0, 640), (640, 640)), ((1280, 640), (1920, 640)), ((2560, 640), (3200, 512)))
MIX_COLS = (((0, 768), (768, 512)), ((1280, 768), (2048, 512)), ((2560, 512), (3072, 512)))
ORDERS = (("z", "y", "x"), ("y", "x", "z"), ("x", "z", "y"))


def layer_kernel(
    lengths_ref,
    residual_ref,
    gain_ref,
    ids_ref,
    gate_values_ref,
    query_hbm,
    query_rope_hbm,
    cache_hbm,
    cache_rope_hbm,
    value_hbm,
    proj_hbm,
    gate_hbm,
    up_hbm,
    down_hbm,
    out_ref,
    query,
    query_rope,
    cache,
    cache_rope,
    scores,
    probs,
    latent_all,
    latent_out,
    latent_in,
    value_up,
    even_part,
    odd_part,
    proj,
    w_gate,
    w_up,
    w_down,
    values,
    attn_sum,
    attn_land0a,
    attn_land0b,
    attn_land1,
    attn_land2,
    residual_out,
    residual_in,
    gates_out,
    gates_in,
    square_out,
    square_in,
    stream,
    swap_out,
    swap_in,
    rows,
    gate_acc,
    up_acc,
    active,
    mix_sum,
    mix_land0,
    mix_land1,
    mix_land2,
    cache_sem,
    load_sem,
    latent_send,
    latent_recv,
    send_sem,
    recv_sem,
):
    group = lax.axis_index("group")
    x_lo = lax.axis_index("dev_1")
    core = lax.axis_index("dev_3")
    pos = {"z": lax.axis_index("dev_0"), "y": lax.axis_index("dev_2"), "x": 2 * group + x_lo}
    other = 1 - core
    first_core = core == 0

    def above(dim):
        return lax.rem(pos[dim] + 1, 4)

    def below(dim):
        return lax.rem(pos[dim] + 3, 4)

    def across(dim):
        return lax.rem(pos[dim] + 2, 4)

    def device(dim, place):
        if dim == "z":
            return {"dev_0": place}
        if dim == "y":
            return {"dev_2": place}
        return {"group": lax.div(place, 2), "dev_1": lax.rem(place, 2)}

    partner = {"dev_3": other}
    x_pair = {"dev_1": 1 - x_lo}
    sent = []

    def send(src, dst, to):
        number = len(sent)
        copy = pltpu.make_async_remote_copy(
            src_ref=src,
            dst_ref=dst,
            send_sem=send_sem.at[number],
            recv_sem=recv_sem.at[number],
            device_id=to,
            device_id_type=MESH,
        )
        copy.start()
        sent.append(copy)
        return copy

    def load(number, src, dst):
        copy = pltpu.make_async_copy(src, dst, load_sem.at[number])
        copy.start()
        return copy

    def load_cache(token):
        slot = token % 2
        copy = pltpu.make_async_copy(cache_hbm.at[token], cache.at[slot], cache_sem.at[slot])
        copy.start()
        return copy

    query_load = load(4, query_hbm, query)
    query_rope_load = load(5, query_rope_hbm, query_rope)
    cache_loads = [load_cache(0)]
    cache_rope_load = load(6, cache_rope_hbm, cache_rope)
    cache_loads.append(load_cache(1))

    place = ((pos["z"] * 2 + x_lo) * 4 + pos["y"]) * 2 + core

    def peer(step):
        number = lax.rem(place + step, 64)
        return number, {
            "dev_0": lax.div(number, 16),
            "dev_1": lax.rem(lax.div(number, 8), 2),
            "dev_2": lax.rem(lax.div(number, 2), 4),
            "dev_3": lax.rem(number, 2),
        }

    barrier = pltpu.get_barrier_semaphore()

    def greet(step, carry):
        pl.semaphore_signal(barrier, inc=1, device_id=peer(step)[1], device_id_type=MESH)
        return carry

    lax.fori_loop(1, 64, greet, 0)
    for far_x in (lax.rem(pos["x"] + 3 + 2 * x_lo, 4), across("x")):
        pl.semaphore_signal(barrier, inc=1, device_id=device("x", far_x), device_id_type=MESH)

    own_half = pl.ds(pl.multiple_of(core * HALF, 128), HALF)
    other_half = pl.ds(pl.multiple_of(other * HALF, 128), HALF)
    own_rows = pl.ds(pl.multiple_of(core * 256, 256), 256)
    residual_out[...] = residual_ref[:, other_half]
    lane = lax.broadcasted_iota(jnp.int32, (4, 128), 1)
    gates = jnp.zeros((4, 128), jnp.float32)
    for choice in range(8):
        named = lax.rem(lane, 32) == ids_ref[:, choice : choice + 1]
        gates = gates + jnp.where(named, gate_values_ref[:, choice : choice + 1], 0.0)
    gates_out[...] = gates

    def eight_rows(mine, theirs):
        return jnp.concatenate(
            [jnp.where(first_core, mine, theirs), jnp.where(first_core, theirs, mine)], axis=0
        )

    query_load.wait()
    query_rope_load.wait()
    loads = {}
    for token in range(4):
        slot = token % 2
        cache_loads[token].wait()
        if token == 0:
            cache_rope_load.wait()
            loads["value"] = load(7, value_hbm, value_up)
            loads["proj"] = load(0, proj_hbm.at[:, own_half], proj.at[own_rows])
        length = lengths_ref[token]
        peak = jnp.full((128, 1), -jnp.inf, jnp.float32)
        for start in range(0, 2048, 512):
            cols = pl.ds(start, 512)
            part = lax.dot_general(
                query[token],
                cache[slot, cols, :],
                (((1,), (1,)), ((), ())),
                preferred_element_type=jnp.float32,
            ) + lax.dot_general(
                query_rope[token],
                cache_rope[token, :, cols],
                (((0,), (0,)), ((), ())),
                preferred_element_type=jnp.float32,
            )
            slots = lax.broadcasted_iota(jnp.int32, part.shape, 1) + start
            part = jnp.where(slots < length, part, -jnp.inf)
            scores[:, cols] = part
            peak = jnp.maximum(peak, jnp.max(part, axis=1, keepdims=True))
        total = jnp.zeros((128, 1), jnp.float32)
        for start in range(0, 2048, 512):
            cols = pl.ds(start, 512)
            weights = jnp.exp((scores[:, cols] - peak) * softmax_scale)
            total = total + jnp.sum(weights, axis=1, keepdims=True)
            probs[:, cols] = weights.astype(jnp.bfloat16)
        mixed = jnp.dot(probs[...], cache[slot], preferred_element_type=jnp.float32) / total
        latent_all[:, 2 * token : 2 * token + 2, :] = mixed.reshape(64, 2, 512)
        if token + 2 < 4:
            cache_loads.append(load_cache(token + 2))
        if token == 0:
            pl.semaphore_wait(barrier, 65)
            handed = {
                "residual": send(residual_out, residual_in, partner),
                "gates": send(gates_out, gates_in, partner),
                "proj": send(proj_hbm.at[:, other_half], proj.at[own_rows], partner),
            }
        elif token == 1:
            loads["gate"] = load(1, gate_hbm, w_gate)
        elif token == 2:
            loads["up"] = load(2, up_hbm, w_up)
            loads["down"] = load(3, down_hbm.at[:, own_half], w_down.at[own_rows])
            handed["down"] = send(down_hbm.at[:, other_half], w_down.at[own_rows], partner)

    latent_out[...] = latent_all[...].astype(jnp.bfloat16)

    def scatter(step, carry):
        number, to = peer(lax.rem(step * 19, 64))
        pltpu.make_async_remote_copy(
            src_ref=latent_out.at[number],
            dst_ref=latent_in.at[place],
            send_sem=latent_send.at[0],
            recv_sem=latent_recv.at[0],
            device_id=to,
            device_id_type=MESH,
        ).start()
        return carry

    lax.fori_loop(1, 64, scatter, 0)
    latent_in[place] = latent_out[place]
    latent_copies = pltpu.make_async_remote_copy(
        src_ref=latent_out.at[pl.ds(0, 63)],
        dst_ref=latent_in.at[pl.ds(0, 63)],
        send_sem=latent_send.at[0],
        recv_sem=latent_recv.at[0],
        device_id=partner,
        device_id_type=MESH,
    )

    loads["value"].wait()
    latent_copies.wait_recv()
    latents = latent_in[...].reshape(512, 512)
    even_part[...] = jnp.dot(latents, value_up[0], preferred_element_type=jnp.float32)
    odd_part[...] = jnp.dot(latents, value_up[1], preferred_element_type=jnp.float32)
    values[core] = jnp.concatenate(
        [even_part[pl.ds(0, 256, stride=2), :], odd_part[pl.ds(1, 256, stride=2), :]], axis=1
    ).astype(jnp.bfloat16)

    def ring_start(dim, block, land, cols, part):
        first, second = cols
        up, down = device(dim, above(dim)), device(dim, below(dim))
        if part == 0:
            return (
                send(block(across(dim), first), land(0, first), up),
                send(block(below(dim), first), land(1, first), down),
            )
        return (
            send(block(across(dim), second), land(2, second), down),
            send(block(above(dim), second), land(3, second), up),
        )

    def add_into(target, *terms):
        total = target[...].astype(jnp.float32)
        for term in terms:
            total = total + term[...].astype(jnp.float32)
        return total

    def ring_relay(dim, block, land, cols, started):
        first, second = cols
        up, down = device(dim, above(dim)), device(dim, below(dim))
        started[0][0].wait_recv()
        target = block(above(dim), first)
        target[...] = add_into(target, land(0, first)).astype(jnp.bfloat16)
        upward = send(target, land(4, first), up)
        started[1][0].wait_recv()
        target = block(below(dim), second)
        target[...] = add_into(target, land(2, second)).astype(jnp.bfloat16)
        downward = send(target, land(5, second), down)
        return upward, downward

    def ring_finish(dim, block, land, cols, started, relayed, store):
        first, second = cols
        started[0][1].wait_recv()
        relayed[0].wait_recv()
        store(first, add_into(block(pos[dim], first), land(1, first), land(4, first)))
        started[1][1].wait_recv()
        relayed[1].wait_recv()
        store(second, add_into(block(pos[dim], second), land(3, second), land(5, second)))

    def direct_start(dim, block, land, cols):
        return [
            send(block(where(dim), cols), land(slot, cols), device(dim, where(dim)))
            for slot, where in enumerate((above, below, across))
        ]

    def direct_finish(dim, block, land, cols, started, store):
        for copy in started:
            copy.wait_recv()
        store(cols, add_into(block(pos[dim], cols), *(land(slot, cols) for slot in range(3))))

    def whole_cols(cols):
        return cols[0][0], cols[0][1] + cols[1][1]

    def span(cols):
        return pl.ds(cols[0], cols[1])

    handed["values"] = send(values.at[core], values.at[core], partner)

    def attn_block(rotation, phase):
        dims = ATTN_ORDERS[rotation]

        def block(place, cols):
            at = {}
            for earlier in dims[:phase]:
                at[earlier] = pos[earlier]
            at[dims[phase]] = place
            return attn_sum.at[
                at.get("z", slice(None)), slice(None), at.get("y", slice(None)), slice(None), span(cols)
            ]

        return block

    def attn_land(rotation, phase):
        if phase == 0:
            land = (attn_land0a, attn_land0b)[rotation]
            return lambda slot, cols: land.at[
                slot, slice(None), slice(None), slice(None), pl.ds(0, cols[1])
            ]
        return lambda slot, cols: attn_land1.at[
            rotation, slot, slice(None), slice(None), pl.ds(0, cols[1])
        ]

    started = {}
    loads["proj"].wait()
    handed["proj"].wait_recv()
    handed["values"].wait_recv()
    for rotation in range(2):
        for part in range(2):
            cols = ATTN_COLS[rotation][part]
            for start in range(cols[0], cols[0] + cols[1], UNIT):
                piece = pl.ds(start, UNIT)
                share = jnp.dot(
                    values[0], proj[0:256, piece], preferred_element_type=jnp.float32
                ) + jnp.dot(values[1], proj[256:512, piece], preferred_element_type=jnp.float32)
                attn_sum[:, :, :, :, piece] = share.reshape(4, 2, 4, 8, UNIT).astype(jnp.bfloat16)
            started[rotation, part] = ring_start(
                ATTN_ORDERS[rotation][0],
                attn_block(rotation, 0),
                attn_land(rotation, 0),
                ATTN_COLS[rotation],
                part,
            )
    relayed = {}
    for rotation in range(2):
        relayed[rotation] = ring_relay(
            ATTN_ORDERS[rotation][0],
            attn_block(rotation, 0),
            attn_land(rotation, 0),
            ATTN_COLS[rotation],
            (started[rotation, 0], started[rotation, 1]),
        )

    def keep_in(block, dim):
        def store(cols, total):
            block(pos[dim], cols)[...] = total.astype(jnp.bfloat16)

        return store

    for rotation in range(2):
        dim, next_dim = ATTN_ORDERS[rotation]
        block = attn_block(rotation, 0)
        ring_finish(
            dim,
            block,
            attn_land(rotation, 0),
            ATTN_COLS[rotation],
            (started[rotation, 0], started[rotation, 1]),
            relayed[rotation],
            keep_in(block, dim),
        )
        started[rotation] = direct_start(
            next_dim, attn_block(rotation, 1), attn_land(rotation, 1), whole_cols(ATTN_COLS[rotation])
        )
    paired = {}
    for rotation in range(2):
        dim = ATTN_ORDERS[rotation][1]
        block = attn_block(rotation, 1)
        cols = whole_cols(ATTN_COLS[rotation])
        direct_finish(
            dim, block, attn_land(rotation, 1), cols, started[rotation], keep_in(block, dim)
        )
        paired[rotation] = send(
            attn_sum.at[pos["z"], 1 - x_lo, pos["y"], slice(None), span(cols)],
            attn_land2.at[slice(None), span(cols)],
            x_pair,
        )
    handed["residual"].wait_recv()
    handed["gates"].wait_recv()
    for rotation in range(2):
        paired[rotation].wait_recv()
    residual = eight_rows(
        residual_ref[:, own_half].astype(jnp.float32), residual_in[...].astype(jnp.float32)
    )
    stream[...] = (
        residual
        + attn_sum[pos["z"], x_lo, pos["y"]].astype(jnp.float32)
        + attn_land2[...].astype(jnp.float32)
    )
    square = jnp.sum(stream[...] * stream[...], axis=1, keepdims=True)
    square_out[...] = jnp.broadcast_to(square, (8, 128))
    squared = send(square_out, square_in, partner)
    dense = eight_rows(gates_out[...], gates_in[...])
    coarse = dense.astype(jnp.bfloat16).astype(jnp.float32)
    lane = lax.broadcasted_iota(jnp.int32, dense.shape, 1)
    packed = jnp.where(lane < 32, coarse, jnp.where(lane < 64, dense - coarse, 0.0))
    mine = (core, pos["x"], pos["y"], pos["z"])
    rows[mine + (slice(None), pl.ds(HALF, 128))] = packed.astype(jnp.bfloat16)
    squared.wait_recv()
    total = square_out[:, 0:1] + square_in[:, 0:1]
    scale = lax.rsqrt(total / (2 * HALF) + 1e-06)
    rows[mine + (slice(None), pl.ds(0, HALF))] = (
        stream[...] * scale * gain_ref[:, own_half]
    ).astype(jnp.bfloat16)

    def row_block(at, cols):
        return rows.at[
            core,
            at.get("x", slice(None)),
            at.get("y", slice(None)),
            at.get("z", slice(None)),
            slice(None),
            span(cols),
        ]

    shared = []
    opened = {}
    for rotation in range(3):
        dim = ORDERS[rotation][0]
        own = row_block(pos, whole_cols(GATHER_COLS[rotation]))
        opened[rotation] = [
            send(own, own, device(dim, where(dim))) for where in (above, below, across)
        ]
    for rotation in range(3):
        for copy in opened[rotation]:
            copy.wait_recv()
    for phase in range(1, 3):
        opened = {}
        for rotation in range(3):
            dims = ORDERS[rotation]
            dim = dims[phase]
            first, second = GATHER_COLS[rotation]
            fixed = {later: pos[later] for later in dims[phase:]}
            up, down = device(dim, above(dim)), device(dim, below(dim))
            one, two = row_block(fixed, first), row_block(fixed, second)
            opened[rotation] = (
                send(one, one, up),
                send(two, two, down),
                send(two, two, up),
                send(one, one, down),
            )
            if phase == 2:
                whole = row_block(fixed, (first[0], first[1] + second[1]))
                shared.append(send(whole, whole, partner))
        forwarded = {}
        for rotation in range(3):
            dims = ORDERS[rotation]
            dim = dims[phase]
            first, second = GATHER_COLS[rotation]
            fixed = {later: pos[later] for later in dims[phase:]}
            up, down = device(dim, above(dim)), device(dim, below(dim))
            opened[rotation][0].wait_recv()
            one = row_block({**fixed, dim: below(dim)}, first)
            opened[rotation][1].wait_recv()
            two = row_block({**fixed, dim: above(dim)}, second)
            forwarded[rotation] = (send(one, one, up), send(two, two, down))
        for rotation in range(3):
            dims = ORDERS[rotation]
            dim = dims[phase]
            first, second = GATHER_COLS[rotation]
            fixed = {later: pos[later] for later in dims[phase:]}
            opened[rotation][2].wait_recv()
            opened[rotation][3].wait_recv()
            if phase == 2:
                for place in (below(dim), above(dim)):
                    whole = row_block({**fixed, dim: place}, (first[0], first[1] + second[1]))
                    shared.append(send(whole, whole, partner))
        for rotation in range(3):
            dims = ORDERS[rotation]
            dim = dims[phase]
            first, second = GATHER_COLS[rotation]
            fixed = {later: pos[later] for later in dims[phase:]}
            forwarded[rotation][0].wait_recv()
            forwarded[rotation][1].wait_recv()
            if phase == 2:
                whole = row_block({**fixed, dim: across(dim)}, (first[0], first[1] + second[1]))
                shared.append(send(whole, whole, partner))
    for copy in shared:
        copy.wait_recv()

    loads["gate"].wait()
    loads["up"].wait()
    gate_acc[...] = jnp.zeros_like(gate_acc)
    up_acc[...] = jnp.zeros_like(up_acc)
    depth = 512
    for half in range(2):

        def product(step, carry):
            at = pl.multiple_of(step * depth, depth)
            row = pl.multiple_of(half * HALF + step * depth, depth)
            lhs = rows[half, :, :, :, :, pl.ds(at, depth)].reshape(512, depth)
            gate_acc[...] += jnp.dot(
                lhs, w_gate[pl.ds(row, depth), :], preferred_element_type=jnp.float32
            )
            up_acc[...] += jnp.dot(
                lhs, w_up[pl.ds(row, depth), :], preferred_element_type=jnp.float32
            )
            return carry

        lax.fori_loop(0, HALF // depth, product, 0)
    expert = (pos["z"] * 2 + x_lo) * 4 + pos["y"]
    parts = rows[0, :, :, :, :, HALF : HALF + 128].astype(jnp.float32).reshape(512, 128)
    lane = lax.broadcasted_iota(jnp.int32, parts.shape, 1)
    picked = jnp.where((lane == expert) | (lane == expert + 32), parts, 0.0)
    row_gate = jnp.sum(picked, axis=1, keepdims=True)
    gate_part = gate_acc[...]
    active[core] = (gate_part * jax.nn.sigmoid(gate_part) * up_acc[...] * row_gate).astype(
        jnp.bfloat16
    )

    handed["active"] = send(active.at[core], active.at[core], partner)
    loads["down"].wait()
    handed["down"].wait_recv()
    handed["active"].wait_recv()

    def mix_block(rotation, phase):
        dims = ORDERS[rotation][::-1]

        def block(place, cols):
            at = {}
            for earlier in dims[:phase]:
                at[earlier] = pos[earlier]
            at[dims[phase]] = place
            return mix_sum.at[
                at.get("x", slice(None)),
                at.get("y", slice(None)),
                at.get("z", slice(None)),
                slice(None),
                span(cols),
            ]

        return block

    def mix_land(rotation, phase):
        land = (mix_land0, mix_land1, mix_land2)[phase]

        def place(slot, cols):
            return land.at[
                (rotation, slot) + (slice(None),) * (3 - phase) + (pl.ds(0, cols[1]),)
            ]

        return place

    started = {}
    for rotation in range(3):
        for part in range(2):
            cols = MIX_COLS[rotation][part]
            for start in range(cols[0], cols[0] + cols[1], UNIT):
                piece = pl.ds(start, UNIT)
                share = jnp.dot(
                    active[0], w_down[0:256, piece], preferred_element_type=jnp.float32
                ) + jnp.dot(active[1], w_down[256:512, piece], preferred_element_type=jnp.float32)
                mix_sum[:, :, :, :, piece] = share.reshape(4, 4, 4, 8, UNIT).astype(jnp.bfloat16)
            started[rotation, part] = ring_start(
                ORDERS[rotation][2], mix_block(rotation, 0), mix_land(rotation, 0), MIX_COLS[rotation], part
            )
    for phase in range(2):
        relayed = {}
        for rotation in range(3):
            relayed[rotation] = ring_relay(
                ORDERS[rotation][2 - phase],
                mix_block(rotation, phase),
                mix_land(rotation, phase),
                MIX_COLS[rotation],
                (started[rotation, 0], started[rotation, 1]),
            )
        for rotation in range(3):
            dim = ORDERS[rotation][2 - phase]
            block = mix_block(rotation, phase)
            ring_finish(
                dim,
                block,
                mix_land(rotation, phase),
                MIX_COLS[rotation],
                (started[rotation, 0], started[rotation, 1]),
                relayed[rotation],
                keep_in(block, dim),
            )
            if phase == 0:
                for part in range(2):
                    started[rotation, part] = ring_start(
                        ORDERS[rotation][1],
                        mix_block(rotation, 1),
                        mix_land(rotation, 1),
                        MIX_COLS[rotation],
                        part,
                    )
            else:
                started[rotation] = direct_start(
                    ORDERS[rotation][0],
                    mix_block(rotation, 2),
                    mix_land(rotation, 2),
                    whole_cols(MIX_COLS[rotation]),
                )

    def add_to_stream(cols, total):
        stream[:, span(cols)] += total

    for rotation in range(3):
        direct_finish(
            ORDERS[rotation][0],
            mix_block(rotation, 2),
            mix_land(rotation, 2),
            whole_cols(MIX_COLS[rotation]),
            started[rotation],
            add_to_stream,
        )
    top, bottom = stream[0:4, :], stream[4:8, :]
    swap_out[...] = jnp.where(first_core, bottom, top)
    swapped = send(swap_out, swap_in, partner)
    mine = jnp.where(first_core, top, bottom)
    swapped.wait_recv()
    theirs = swap_in[...]
    out_ref[:, 0:HALF] = jnp.where(first_core, mine, theirs).astype(jnp.bfloat16)
    out_ref[:, HALF : 2 * HALF] = jnp.where(first_core, theirs, mine).astype(jnp.bfloat16)
    for copy in sent:
        copy.wait_send()
    latent_copies.wait_send()


def layer(
    lengths,
    residual,
    norm_gain,
    expert_ids,
    gate_values,
    query_latent,
    query_rope,
    cache_latent,
    cache_rope,
    value_up,
    out_proj,
    w_gate,
    w_up,
    w_down,
):
    bf16, f32 = jnp.bfloat16, jnp.float32
    vmem = pl.BlockSpec(memory_space=pltpu.VMEM)
    hbm = pl.BlockSpec(memory_space=pl.ANY)
    return pl.pallas_call(
        layer_kernel,
        out_shape=jax.ShapeDtypeStruct((4, 2 * HALF), bf16),
        in_specs=[pl.BlockSpec(memory_space=pltpu.SMEM)] + [vmem] * 4 + [hbm] * 9,
        out_specs=vmem,
        scratch_shapes=[
            pltpu.VMEM(query_latent.shape, bf16),
            pltpu.VMEM(query_rope.shape, bf16),
            pltpu.VMEM((2, 2048, 512), bf16),
            pltpu.VMEM(cache_rope.shape, bf16),
            pltpu.VMEM((128, 2048), f32),
            pltpu.VMEM((128, 2048), bf16),
            pltpu.VMEM((64, 8, 512), f32),
            pltpu.VMEM((64, 8, 512), bf16),
            pltpu.VMEM((64, 8, 512), bf16),
            pltpu.VMEM(value_up.shape, bf16),
            pltpu.VMEM((512, 128), f32),
            pltpu.VMEM((512, 128), f32),
            pltpu.VMEM((512, HALF), bf16),
            pltpu.VMEM(w_gate.shape, bf16),
            pltpu.VMEM(w_up.shape, bf16),
            pltpu.VMEM((512, HALF), bf16),
            pltpu.VMEM((2, 256, 256), bf16),
            pltpu.VMEM((4, 2, 4, 8, HALF), bf16),
            pltpu.VMEM((6, 2, 4, 8, 1024), bf16),
            pltpu.VMEM((6, 4, 2, 8, 1024), bf16),
            pltpu.VMEM((2, 3, 2, 8, 1792), bf16),
            pltpu.VMEM((8, HALF), bf16),
            pltpu.VMEM((4, HALF), bf16),
            pltpu.VMEM((4, HALF), bf16),
            pltpu.VMEM((4, 128), f32),
            pltpu.VMEM((4, 128), f32),
            pltpu.VMEM((8, 128), f32),
            pltpu.VMEM((8, 128), f32),
            pltpu.VMEM((8, HALF), f32),
            pltpu.VMEM((4, HALF), f32),
            pltpu.VMEM((4, HALF), f32),
            pltpu.VMEM((2, 4, 4, 4, 8, HALF + 128), bf16),
            pltpu.VMEM((512, 256), f32),
            pltpu.VMEM((512, 256), f32),
            pltpu.VMEM((2, 512, 256), bf16),
            pltpu.VMEM((4, 4, 4, 8, HALF), bf16),
            pltpu.VMEM((3, 6, 4, 4, 8, 768), bf16),
            pltpu.VMEM((3, 6, 4, 8, 768), bf16),
            pltpu.VMEM((3, 3, 8, 1280), bf16),
            pltpu.SemaphoreType.DMA((2,)),
            pltpu.SemaphoreType.DMA((8,)),
            pltpu.SemaphoreType.DMA((1,)),
            pltpu.SemaphoreType.DMA((1,)),
            pltpu.SemaphoreType.DMA((170,)),
            pltpu.SemaphoreType.DMA((170,)),
        ],
        compiler_params=pltpu.CompilerParams(
            collective_id=0, has_side_effects=True, vmem_limit_bytes=63 * 1024 * 1024
        ),
    )(
        lengths,
        residual,
        norm_gain,
        expert_ids,
        gate_values,
        query_latent,
        query_rope,
        cache_latent,
        cache_rope,
        value_up,
        out_proj,
        w_gate,
        w_up,
        w_down,
    )


def local(
    query_latent,
    query_rope,
    cache_latent,
    cache_rope,
    lengths,
    value_up,
    out_proj,
    residual,
    norm_gain,
    expert_ids,
    gate_values,
    w_gate,
    w_up,
    w_down,
):
    return layer(
        lengths,
        residual,
        norm_gain[None, :],
        expert_ids,
        gate_values,
        query_latent,
        jnp.swapaxes(query_rope, 1, 2),
        cache_latent,
        cache_rope,
        value_up,
        out_proj,
        w_gate[0],
        w_up[0],
        w_down[0],
    )


def solution(mesh):
    finer = Mesh(
        mesh.devices.reshape(mesh.shape["group"], 4, 2, 4, 2),
        ("group", "dev_0", "dev_1", "dev_2", "dev_3"),
    )
    return jax.shard_map(
        local,
        mesh=finer,
        in_specs=(
            P(GROUP_DEV, None, None),
            P(GROUP_DEV, None, None),
            P(GROUP_DEV, None, None),
            P(GROUP_DEV, None, None),
            P(GROUP_DEV),
            P(DEV, None, None),
            P(DEV, None),
            P(GROUP_DEV, None),
            P(),
            P(GROUP_DEV, None),
            P(GROUP_DEV, None),
            P(DEV, None, "group"),
            P(DEV, None, "group"),
            P(DEV, "group", None),
        ),
        out_specs=P(GROUP_DEV, None),
        check_vma=False,
    )
```

```python
import functools

import jax
import jax.numpy as jnp
from jax import lax
from jax.experimental import pallas as pl
from jax.experimental.pallas import tpu as pltpu
from jax.sharding import Mesh
from jax.sharding import PartitionSpec as P

DEV = ("dev_0", "dev_1", "dev_2", "dev_3")
GROUP_DEV = ("group", "dev_0", "dev_1", "dev_2", "dev_3")
MESH = pl.DeviceIdType.MESH


softmax_scale = 192.0 ** (-0.5)


HALF = 3584
UNIT = 256
ATTN_COLS = (((0, 1024), (1024, 768)), ((1792, 1024), (2816, 768)))
ATTN_ORDERS = (("z", "y"), ("y", "z"))
GATHER_COLS = (((0, 640), (640, 640)), ((1280, 640), (1920, 640)), ((2560, 640), (3200, 512)))
MIX_COLS = (((0, 768), (768, 512)), ((1280, 768), (2048, 512)), ((2560, 512), (3072, 512)))
ORDERS = (("z", "y", "x"), ("y", "x", "z"), ("x", "z", "y"))


def layer_kernel(
    lengths_ref,
    residual_ref,
    gain_ref,
    ids_ref,
    gate_values_ref,
    query_hbm,
    query_rope_hbm,
    cache_hbm,
    cache_rope_hbm,
    value_hbm,
    proj_hbm,
    gate_hbm,
    up_hbm,
    down_hbm,
    out_ref,
    query,
    query_rope,
    cache,
    cache_rope,
    scores,
    probs,
    latent_all,
    latent_out,
    latent_in,
    value_up,
    even_part,
    odd_part,
    even_values,
    odd_values,
    proj,
    w_gate,
    w_up,
    w_down,
    values,
    attn_sum,
    attn_land0a,
    attn_land0b,
    attn_land1,
    attn_land2,
    residual_out,
    residual_in,
    gates_out,
    gates_in,
    square_out,
    square_in,
    stream,
    swap_out,
    swap_in,
    rows,
    gate_acc,
    up_acc,
    active,
    mix_sum,
    mix_land0,
    mix_land1,
    mix_land2,
    cache_sem,
    load_sem,
    latent_send,
    latent_recv,
    send_sem,
    recv_sem,
):
    group = lax.axis_index("group")
    x_lo = lax.axis_index("dev_1")
    core = lax.axis_index("dev_3")
    pos = {"z": lax.axis_index("dev_0"), "y": lax.axis_index("dev_2"), "x": 2 * group + x_lo}
    other = 1 - core
    first_core = core == 0

    def above(dim):
        return lax.rem(pos[dim] + 1, 4)

    def below(dim):
        return lax.rem(pos[dim] + 3, 4)

    def across(dim):
        return lax.rem(pos[dim] + 2, 4)

    def device(dim, place):
        if dim == "z":
            return {"dev_0": place}
        if dim == "y":
            return {"dev_2": place}
        return {"group": lax.div(place, 2), "dev_1": lax.rem(place, 2)}

    partner = {"dev_3": other}
    x_pair = {"dev_1": 1 - x_lo}
    sent = []

    def send(src, dst, to):
        number = len(sent)
        copy = pltpu.make_async_remote_copy(
            src_ref=src,
            dst_ref=dst,
            send_sem=send_sem.at[number],
            recv_sem=recv_sem.at[number],
            device_id=to,
            device_id_type=MESH,
        )
        copy.start()
        sent.append(copy)
        return copy

    def load(number, src, dst):
        copy = pltpu.make_async_copy(src, dst, load_sem.at[number])
        copy.start()
        return copy

    def load_cache(token):
        slot = token % 2
        copy = pltpu.make_async_copy(cache_hbm.at[token], cache.at[slot], cache_sem.at[slot])
        copy.start()
        return copy

    query_load = load(4, query_hbm, query)
    query_rope_load = load(5, query_rope_hbm, query_rope)
    cache_loads = [load_cache(0)]
    cache_rope_load = load(6, cache_rope_hbm, cache_rope)
    cache_loads.append(load_cache(1))

    place = ((pos["z"] * 2 + x_lo) * 4 + pos["y"]) * 2 + core

    def peer(step):
        number = lax.rem(place + step, 64)
        return number, {
            "dev_0": lax.div(number, 16),
            "dev_1": lax.rem(lax.div(number, 8), 2),
            "dev_2": lax.rem(lax.div(number, 2), 4),
            "dev_3": lax.rem(number, 2),
        }

    barrier = pltpu.get_barrier_semaphore()

    def greet(step, carry):
        pl.semaphore_signal(barrier, inc=1, device_id=peer(step)[1], device_id_type=MESH)
        return carry

    lax.fori_loop(1, 64, greet, 0)
    for far_x in (lax.rem(pos["x"] + 3 + 2 * x_lo, 4), across("x")):
        pl.semaphore_signal(barrier, inc=1, device_id=device("x", far_x), device_id_type=MESH)

    own_half = pl.ds(pl.multiple_of(core * HALF, 128), HALF)
    other_half = pl.ds(pl.multiple_of(other * HALF, 128), HALF)
    own_rows = pl.ds(pl.multiple_of(core * 256, 256), 256)
    residual_out[...] = residual_ref[:, other_half]
    lane = lax.broadcasted_iota(jnp.int32, (4, 128), 1)
    gates = jnp.zeros((4, 128), jnp.float32)
    for choice in range(8):
        named = lax.rem(lane, 32) == ids_ref[:, choice : choice + 1]
        gates = gates + jnp.where(named, gate_values_ref[:, choice : choice + 1], 0.0)
    gates_out[...] = gates

    def eight_rows(mine, theirs):
        return jnp.concatenate(
            [jnp.where(first_core, mine, theirs), jnp.where(first_core, theirs, mine)], axis=0
        )

    def scatter_pair(pair):
        latent_out[pair] = latent_all[...].astype(jnp.bfloat16)

        def scatter(step, carry):
            number, to = peer(lax.rem(step * 19, 64))
            pltpu.make_async_remote_copy(
                src_ref=latent_out.at[pair, number],
                dst_ref=latent_in.at[pair, place],
                send_sem=latent_send.at[pair],
                recv_sem=latent_recv.at[pair],
                device_id=to,
                device_id_type=MESH,
            ).start()
            return carry

        lax.fori_loop(1, 64, scatter, 0)
        latent_in[pair, place] = latent_out[pair, place]

    def latent_copies(pair):
        return pltpu.make_async_remote_copy(
            src_ref=latent_out.at[pair, pl.ds(0, 63)],
            dst_ref=latent_in.at[pair, pl.ds(0, 63)],
            send_sem=latent_send.at[pair],
            recv_sem=latent_recv.at[pair],
            device_id=partner,
            device_id_type=MESH,
        )

    query_load.wait()
    query_rope_load.wait()
    loads = {}
    for token in range(4):
        slot = token % 2
        cache_loads[token].wait()
        if token == 0:
            cache_rope_load.wait()
            loads["value"] = load(7, value_hbm, value_up)
            loads["proj"] = load(0, proj_hbm.at[:, own_half], proj.at[own_rows])
        length = lengths_ref[token]
        peak = jnp.full((128, 1), -jnp.inf, jnp.float32)
        for start in range(0, 2048, 512):
            cols = pl.ds(start, 512)
            part = lax.dot_general(
                query[token],
                cache[slot, cols, :],
                (((1,), (1,)), ((), ())),
                preferred_element_type=jnp.float32,
            ) + lax.dot_general(
                query_rope[token],
                cache_rope[token, :, cols],
                (((0,), (0,)), ((), ())),
                preferred_element_type=jnp.float32,
            )
            slots = lax.broadcasted_iota(jnp.int32, part.shape, 1) + start
            part = jnp.where(slots < length, part, -jnp.inf)
            scores[:, cols] = part
            peak = jnp.maximum(peak, jnp.max(part, axis=1, keepdims=True))
        total = jnp.zeros((128, 1), jnp.float32)
        for start in range(0, 2048, 512):
            cols = pl.ds(start, 512)
            weights = jnp.exp((scores[:, cols] - peak) * softmax_scale)
            total = total + jnp.sum(weights, axis=1, keepdims=True)
            probs[:, cols] = weights.astype(jnp.bfloat16)
        mixed = jnp.dot(probs[...], cache[slot], preferred_element_type=jnp.float32) / total
        latent_all[:, 2 * slot : 2 * slot + 2, :] = mixed.reshape(64, 2, 512)
        if token + 2 < 4:
            cache_loads.append(load_cache(token + 2))
        if token == 0:
            pl.semaphore_wait(barrier, 65)
            handed = {
                "residual": send(residual_out, residual_in, partner),
                "gates": send(gates_out, gates_in, partner),
                "proj": send(proj_hbm.at[:, other_half], proj.at[own_rows], partner),
            }
        elif token == 1:
            loads["gate"] = load(1, gate_hbm, w_gate)
        elif token == 2:
            loads["up"] = load(2, up_hbm, w_up)
            loads["down"] = load(3, down_hbm.at[:, own_half], w_down.at[own_rows])
            handed["down"] = send(down_hbm.at[:, other_half], w_down.at[own_rows], partner)
        if token % 2 == 1:
            scatter_pair(token // 2)

    loads["value"].wait()
    for pair in range(2):
        latent_copies(pair).wait_recv()
        latents = latent_in[pair].reshape(256, 512)
        even_part[...] = jnp.dot(latents, value_up[0], preferred_element_type=jnp.float32)
        odd_part[...] = jnp.dot(latents, value_up[1], preferred_element_type=jnp.float32)
        for part, kept in ((even_part, even_values), (odd_part, odd_values)):
            first = 0 if part is even_part else 1
            heads = part[pl.ds(first, 128, stride=2), :].reshape(32, 2, 2, 128)
            for owner in range(2):
                at = 4 * owner + 2 * pair
                kept[:, at : at + 2, :] = heads[:, owner]
    values[core] = jnp.concatenate(
        [even_values[...].reshape(256, 128), odd_values[...].reshape(256, 128)], axis=1
    ).astype(jnp.bfloat16)

    def ring_start(dim, block, land, cols, part):
        first, second = cols
        up, down = device(dim, above(dim)), device(dim, below(dim))
        if part == 0:
            return (
                send(block(across(dim), first), land(0, first), up),
                send(block(below(dim), first), land(1, first), down),
            )
        return (
            send(block(across(dim), second), land(2, second), down),
            send(block(above(dim), second), land(3, second), up),
        )

    def add_into(target, *terms):
        total = target[...].astype(jnp.float32)
        for term in terms:
            total = total + term[...].astype(jnp.float32)
        return total

    def ring_relay(dim, block, land, cols, started):
        first, second = cols
        up, down = device(dim, above(dim)), device(dim, below(dim))
        started[0][0].wait_recv()
        target = block(above(dim), first)
        target[...] = add_into(target, land(0, first)).astype(jnp.bfloat16)
        upward = send(target, land(4, first), up)
        started[1][0].wait_recv()
        target = block(below(dim), second)
        target[...] = add_into(target, land(2, second)).astype(jnp.bfloat16)
        downward = send(target, land(5, second), down)
        return upward, downward

    def ring_finish(dim, block, land, cols, started, relayed, store):
        first, second = cols
        started[0][1].wait_recv()
        relayed[0].wait_recv()
        store(first, add_into(block(pos[dim], first), land(1, first), land(4, first)))
        started[1][1].wait_recv()
        relayed[1].wait_recv()
        store(second, add_into(block(pos[dim], second), land(3, second), land(5, second)))

    def direct_start(dim, block, land, cols):
        return [
            send(block(where(dim), cols), land(slot, cols), device(dim, where(dim)))
            for slot, where in enumerate((above, below, across))
        ]

    def direct_finish(dim, block, land, cols, started, store):
        for copy in started:
            copy.wait_recv()
        store(cols, add_into(block(pos[dim], cols), *(land(slot, cols) for slot in range(3))))

    def whole_cols(cols):
        return cols[0][0], cols[0][1] + cols[1][1]

    def span(cols):
        return pl.ds(cols[0], cols[1])

    handed["values"] = send(values.at[core], values.at[core], partner)

    def attn_block(rotation, phase):
        dims = ATTN_ORDERS[rotation]

        def block(place, cols):
            at = {}
            for earlier in dims[:phase]:
                at[earlier] = pos[earlier]
            at[dims[phase]] = place
            return attn_sum.at[
                at.get("z", slice(None)), slice(None), at.get("y", slice(None)), slice(None), span(cols)
            ]

        return block

    def attn_land(rotation, phase):
        if phase == 0:
            land = (attn_land0a, attn_land0b)[rotation]
            return lambda slot, cols: land.at[
                slot, slice(None), slice(None), slice(None), pl.ds(0, cols[1])
            ]
        return lambda slot, cols: attn_land1.at[
            rotation, slot, slice(None), slice(None), pl.ds(0, cols[1])
        ]

    started = {}
    loads["proj"].wait()
    handed["proj"].wait_recv()
    handed["values"].wait_recv()
    for rotation in range(2):
        for part in range(2):
            cols = ATTN_COLS[rotation][part]
            for start in range(cols[0], cols[0] + cols[1], UNIT):
                piece = pl.ds(start, UNIT)
                share = jnp.dot(
                    values[0], proj[0:256, piece], preferred_element_type=jnp.float32
                ) + jnp.dot(values[1], proj[256:512, piece], preferred_element_type=jnp.float32)
                attn_sum[:, :, :, :, piece] = share.reshape(4, 2, 4, 8, UNIT).astype(jnp.bfloat16)
            started[rotation, part] = ring_start(
                ATTN_ORDERS[rotation][0],
                attn_block(rotation, 0),
                attn_land(rotation, 0),
                ATTN_COLS[rotation],
                part,
            )
    relayed = {}
    for rotation in range(2):
        relayed[rotation] = ring_relay(
            ATTN_ORDERS[rotation][0],
            attn_block(rotation, 0),
            attn_land(rotation, 0),
            ATTN_COLS[rotation],
            (started[rotation, 0], started[rotation, 1]),
        )

    def keep_in(block, dim):
        def store(cols, total):
            block(pos[dim], cols)[...] = total.astype(jnp.bfloat16)

        return store

    for rotation in range(2):
        dim, next_dim = ATTN_ORDERS[rotation]
        block = attn_block(rotation, 0)
        ring_finish(
            dim,
            block,
            attn_land(rotation, 0),
            ATTN_COLS[rotation],
            (started[rotation, 0], started[rotation, 1]),
            relayed[rotation],
            keep_in(block, dim),
        )
        started[rotation] = direct_start(
            next_dim, attn_block(rotation, 1), attn_land(rotation, 1), whole_cols(ATTN_COLS[rotation])
        )
    paired = {}
    for rotation in range(2):
        dim = ATTN_ORDERS[rotation][1]
        block = attn_block(rotation, 1)
        cols = whole_cols(ATTN_COLS[rotation])
        direct_finish(
            dim, block, attn_land(rotation, 1), cols, started[rotation], keep_in(block, dim)
        )
        paired[rotation] = send(
            attn_sum.at[pos["z"], 1 - x_lo, pos["y"], slice(None), span(cols)],
            attn_land2.at[slice(None), span(cols)],
            x_pair,
        )
    handed["residual"].wait_recv()
    handed["gates"].wait_recv()
    for rotation in range(2):
        paired[rotation].wait_recv()
    residual = eight_rows(
        residual_ref[:, own_half].astype(jnp.float32), residual_in[...].astype(jnp.float32)
    )
    stream[...] = (
        residual
        + attn_sum[pos["z"], x_lo, pos["y"]].astype(jnp.float32)
        + attn_land2[...].astype(jnp.float32)
    )
    square = jnp.sum(stream[...] * stream[...], axis=1, keepdims=True)
    square_out[...] = jnp.broadcast_to(square, (8, 128))
    squared = send(square_out, square_in, partner)
    dense = eight_rows(gates_out[...], gates_in[...])
    coarse = dense.astype(jnp.bfloat16).astype(jnp.float32)
    lane = lax.broadcasted_iota(jnp.int32, dense.shape, 1)
    packed = jnp.where(lane < 32, coarse, jnp.where(lane < 64, dense - coarse, 0.0))
    mine = (core, pos["x"], pos["y"], pos["z"])
    rows[mine + (slice(None), pl.ds(HALF, 128))] = packed.astype(jnp.bfloat16)
    squared.wait_recv()
    total = square_out[:, 0:1] + square_in[:, 0:1]
    scale = lax.rsqrt(total / (2 * HALF) + 1e-06)
    rows[mine + (slice(None), pl.ds(0, HALF))] = (
        stream[...] * scale * gain_ref[:, own_half]
    ).astype(jnp.bfloat16)

    def row_block(at, cols):
        return rows.at[
            core,
            at.get("x", slice(None)),
            at.get("y", slice(None)),
            at.get("z", slice(None)),
            slice(None),
            span(cols),
        ]

    shared = []
    opened = {}
    for rotation in range(3):
        dim = ORDERS[rotation][0]
        own = row_block(pos, whole_cols(GATHER_COLS[rotation]))
        opened[rotation] = [
            send(own, own, device(dim, where(dim))) for where in (above, below, across)
        ]
    for rotation in range(3):
        for copy in opened[rotation]:
            copy.wait_recv()
    def gather_dims(rotation):
        first, second = GATHER_COLS[rotation]
        return ORDERS[rotation], first, second

    def open_ring(dim, at, first, second):
        up, down = device(dim, above(dim)), device(dim, below(dim))
        one, two = row_block(at, first), row_block(at, second)
        return (
            send(one, one, up),
            send(two, two, down),
            send(two, two, up),
            send(one, one, down),
        )

    def forward(dim, at, first, second, begun):
        begun[0].wait_recv()
        one = row_block({**at, dim: below(dim)}, first)
        upward = send(one, one, device(dim, above(dim)))
        begun[1].wait_recv()
        two = row_block({**at, dim: above(dim)}, second)
        return upward, send(two, two, device(dim, below(dim)))

    def hand_over(rotation, at):
        piece = row_block(at, whole_cols(GATHER_COLS[rotation]))
        return send(piece, piece, partner)

    middle, outer, passed, shared = {}, {}, {}, {}
    for rotation in range(3):
        (a, b, c), first, second = gather_dims(rotation)
        middle[rotation] = open_ring(b, {b: pos[b], c: pos[c]}, first, second)
    for rotation in range(3):
        (a, b, c), first, second = gather_dims(rotation)
        at = {b: pos[b], c: pos[c]}
        outer[rotation, "own"] = open_ring(c, at, first, second)
    for rotation in range(3):
        (a, b, c), first, second = gather_dims(rotation)
        passed[rotation] = forward(b, {c: pos[c]}, first, second, middle[rotation])
    for rotation in range(3):
        (a, b, c), first, second = gather_dims(rotation)
        middle[rotation][2].wait_recv()
        middle[rotation][3].wait_recv()
        for where in (below, above):
            outer[rotation, where] = open_ring(c, {b: where(b), c: pos[c]}, first, second)
    onward = {}
    for rotation in range(3):
        (a, b, c), first, second = gather_dims(rotation)
        onward[rotation, "own"] = forward(c, {b: pos[b]}, first, second, outer[rotation, "own"])
    for rotation in range(3):
        (a, b, c), first, second = gather_dims(rotation)
        passed[rotation][0].wait_recv()
        passed[rotation][1].wait_recv()
        outer[rotation, across] = open_ring(c, {b: across(b), c: pos[c]}, first, second)
        shared[rotation, "own"] = [hand_over(rotation, {c: pos[c]})]
    loads["gate"].wait()
    loads["up"].wait()

    def acc_rows(acc, at):
        return acc.at[at.get("x", slice(None)), at.get("y", slice(None)), at.get("z", slice(None))]

    def multiply(half, rotation, at):
        start = GATHER_COLS[rotation][0][0]
        depth = min(whole_cols(GATHER_COLS[rotation])[1], HALF - start)
        index = (at.get("x", slice(None)), at.get("y", slice(None)), at.get("z", slice(None)))
        lhs = rows[(half,) + index + (slice(None), pl.ds(start, depth))].reshape(128, depth)
        weight_rows = pl.ds(pl.multiple_of(half * HALF + start, 128), depth)
        for acc, weight in ((gate_acc, w_gate), (up_acc, w_up)):
            part = jnp.dot(
                lhs, weight[weight_rows, :], preferred_element_type=jnp.float32
            ).reshape(4, 4, 8, 256)
            acc_rows(acc, at)[...] += part

    gate_acc[...] = jnp.zeros_like(gate_acc)
    up_acc[...] = jnp.zeros_like(up_acc)
    for rotation in range(3):
        c = ORDERS[rotation][2]
        multiply(core, rotation, {c: pos[c]})
    for name, where in (("below", below), ("above", above), ("across", across)):
        for rotation in range(3):
            (a, b, c), first, second = gather_dims(rotation)
            onward[rotation, name] = forward(c, {b: where(b)}, first, second, outer[rotation, where])
    for rotation in range(3):
        c = ORDERS[rotation][2]
        shared[rotation, "own"][0].wait_recv()
        multiply(other, rotation, {c: pos[c]})
    for rotation in range(3):
        c = ORDERS[rotation][2]
        for key in ("own", below, above, across):
            outer[rotation, key][2].wait_recv()
            outer[rotation, key][3].wait_recv()
        for where in (below, above):
            shared[rotation, where] = [hand_over(rotation, {c: where(c)})]
    for where in (below, above):
        for rotation in range(3):
            c = ORDERS[rotation][2]
            multiply(core, rotation, {c: where(c)})
    for rotation in range(3):
        b, c = ORDERS[rotation][1:]
        shared[rotation, across] = []
        for name, there in (("own", None), ("below", below), ("above", above), ("across", across)):
            for copy in onward[rotation, name]:
                copy.wait_recv()
            at = {c: across(c), b: pos[b] if there is None else there(b)}
            shared[rotation, across].append(hand_over(rotation, at))
    for where in (below, above):
        for rotation in range(3):
            c = ORDERS[rotation][2]
            shared[rotation, where][0].wait_recv()
            multiply(other, rotation, {c: where(c)})
    for rotation in range(3):
        c = ORDERS[rotation][2]
        multiply(core, rotation, {c: across(c)})
    for rotation in range(3):
        c = ORDERS[rotation][2]
        for copy in shared[rotation, across]:
            copy.wait_recv()
        multiply(other, rotation, {c: across(c)})

    expert = (pos["z"] * 2 + x_lo) * 4 + pos["y"]
    parts = rows[0, :, :, :, :, HALF : HALF + 128].astype(jnp.float32).reshape(512, 128)
    lane = lax.broadcasted_iota(jnp.int32, parts.shape, 1)
    picked = jnp.where((lane == expert) | (lane == expert + 32), parts, 0.0)
    row_gate = jnp.sum(picked, axis=1, keepdims=True)
    gate_part = gate_acc[...].reshape(512, 256)
    active[core] = (gate_part * jax.nn.sigmoid(gate_part) * up_acc[...].reshape(512, 256) * row_gate).astype(
        jnp.bfloat16
    )

    handed["active"] = send(active.at[core], active.at[core], partner)
    loads["down"].wait()
    handed["down"].wait_recv()
    handed["active"].wait_recv()

    def mix_block(rotation, phase):
        dims = ORDERS[rotation][::-1]

        def block(place, cols):
            at = {}
            for earlier in dims[:phase]:
                at[earlier] = pos[earlier]
            at[dims[phase]] = place
            return mix_sum.at[
                at.get("x", slice(None)),
                at.get("y", slice(None)),
                at.get("z", slice(None)),
                slice(None),
                span(cols),
            ]

        return block

    def mix_land(rotation, phase):
        land = (mix_land0, mix_land1, mix_land2)[phase]

        def place(slot, cols):
            return land.at[
                (rotation, slot) + (slice(None),) * (3 - phase) + (pl.ds(0, cols[1]),)
            ]

        return place

    started, relayed = {}, {}

    def mix_relay(rotation, phase):
        relayed[rotation] = ring_relay(
            ORDERS[rotation][2 - phase],
            mix_block(rotation, phase),
            mix_land(rotation, phase),
            MIX_COLS[rotation],
            (started[rotation, 0], started[rotation, 1]),
        )

    for rotation in range(3):
        for part in range(2):
            cols = MIX_COLS[rotation][part]
            for start in range(cols[0], cols[0] + cols[1], UNIT):
                piece = pl.ds(start, UNIT)
                share = jnp.dot(
                    active[0], w_down[0:256, piece], preferred_element_type=jnp.float32
                ) + jnp.dot(active[1], w_down[256:512, piece], preferred_element_type=jnp.float32)
                mix_sum[:, :, :, :, piece] = share.reshape(4, 4, 4, 8, UNIT).astype(jnp.bfloat16)
            started[rotation, part] = ring_start(
                ORDERS[rotation][2], mix_block(rotation, 0), mix_land(rotation, 0), MIX_COLS[rotation], part
            )
        if rotation >= 1:
            mix_relay(rotation - 1, 0)
    mix_relay(2, 0)
    for phase in range(2):
        if phase == 1:
            for rotation in range(3):
                mix_relay(rotation, 1)
        for rotation in range(3):
            dim = ORDERS[rotation][2 - phase]
            block = mix_block(rotation, phase)
            ring_finish(
                dim,
                block,
                mix_land(rotation, phase),
                MIX_COLS[rotation],
                (started[rotation, 0], started[rotation, 1]),
                relayed[rotation],
                keep_in(block, dim),
            )
            if phase == 0:
                for part in range(2):
                    started[rotation, part] = ring_start(
                        ORDERS[rotation][1],
                        mix_block(rotation, 1),
                        mix_land(rotation, 1),
                        MIX_COLS[rotation],
                        part,
                    )
            else:
                started[rotation] = direct_start(
                    ORDERS[rotation][0],
                    mix_block(rotation, 2),
                    mix_land(rotation, 2),
                    whole_cols(MIX_COLS[rotation]),
                )

    def add_to_stream(cols, total):
        stream[:, span(cols)] += total

    for rotation in range(3):
        direct_finish(
            ORDERS[rotation][0],
            mix_block(rotation, 2),
            mix_land(rotation, 2),
            whole_cols(MIX_COLS[rotation]),
            started[rotation],
            add_to_stream,
        )
    top, bottom = stream[0:4, :], stream[4:8, :]
    swap_out[...] = jnp.where(first_core, bottom, top)
    swapped = send(swap_out, swap_in, partner)
    mine = jnp.where(first_core, top, bottom)
    swapped.wait_recv()
    theirs = swap_in[...]
    out_ref[:, 0:HALF] = jnp.where(first_core, mine, theirs).astype(jnp.bfloat16)
    out_ref[:, HALF : 2 * HALF] = jnp.where(first_core, theirs, mine).astype(jnp.bfloat16)
    for copy in sent:
        copy.wait_send()
    for pair in range(2):
        latent_copies(pair).wait_send()


def layer(
    lengths,
    residual,
    norm_gain,
    expert_ids,
    gate_values,
    query_latent,
    query_rope,
    cache_latent,
    cache_rope,
    value_up,
    out_proj,
    w_gate,
    w_up,
    w_down,
):
    bf16, f32 = jnp.bfloat16, jnp.float32
    vmem = pl.BlockSpec(memory_space=pltpu.VMEM)
    hbm = pl.BlockSpec(memory_space=pl.ANY)
    return pl.pallas_call(
        layer_kernel,
        out_shape=jax.ShapeDtypeStruct((4, 2 * HALF), bf16),
        in_specs=[pl.BlockSpec(memory_space=pltpu.SMEM)] + [vmem] * 4 + [hbm] * 9,
        out_specs=vmem,
        scratch_shapes=[
            pltpu.VMEM(query_latent.shape, bf16),
            pltpu.VMEM(query_rope.shape, bf16),
            pltpu.VMEM((2, 2048, 512), bf16),
            pltpu.VMEM(cache_rope.shape, bf16),
            pltpu.VMEM((128, 2048), f32),
            pltpu.VMEM((128, 2048), bf16),
            pltpu.VMEM((64, 4, 512), f32),
            pltpu.VMEM((2, 64, 4, 512), bf16),
            pltpu.VMEM((2, 64, 4, 512), bf16),
            pltpu.VMEM(value_up.shape, bf16),
            pltpu.VMEM((256, 128), f32),
            pltpu.VMEM((256, 128), f32),
            pltpu.VMEM((32, 8, 128), f32),
            pltpu.VMEM((32, 8, 128), f32),
            pltpu.VMEM((512, HALF), bf16),
            pltpu.VMEM(w_gate.shape, bf16),
            pltpu.VMEM(w_up.shape, bf16),
            pltpu.VMEM((512, HALF), bf16),
            pltpu.VMEM((2, 256, 256), bf16),
            pltpu.VMEM((4, 2, 4, 8, HALF), bf16),
            pltpu.VMEM((6, 2, 4, 8, 1024), bf16),
            pltpu.VMEM((6, 4, 2, 8, 1024), bf16),
            pltpu.VMEM((2, 3, 2, 8, 1792), bf16),
            pltpu.VMEM((8, HALF), bf16),
            pltpu.VMEM((4, HALF), bf16),
            pltpu.VMEM((4, HALF), bf16),
            pltpu.VMEM((4, 128), f32),
            pltpu.VMEM((4, 128), f32),
            pltpu.VMEM((8, 128), f32),
            pltpu.VMEM((8, 128), f32),
            pltpu.VMEM((8, HALF), f32),
            pltpu.VMEM((4, HALF), f32),
            pltpu.VMEM((4, HALF), f32),
            pltpu.VMEM((2, 4, 4, 4, 8, HALF + 128), bf16),
            pltpu.VMEM((4, 4, 4, 8, 256), f32),
            pltpu.VMEM((4, 4, 4, 8, 256), f32),
            pltpu.VMEM((2, 512, 256), bf16),
            pltpu.VMEM((4, 4, 4, 8, HALF), bf16),
            pltpu.VMEM((3, 6, 4, 4, 8, 768), bf16),
            pltpu.VMEM((3, 6, 4, 8, 768), bf16),
            pltpu.VMEM((3, 3, 8, 1280), bf16),
            pltpu.SemaphoreType.DMA((2,)),
            pltpu.SemaphoreType.DMA((8,)),
            pltpu.SemaphoreType.DMA((2,)),
            pltpu.SemaphoreType.DMA((2,)),
            pltpu.SemaphoreType.DMA((240,)),
            pltpu.SemaphoreType.DMA((240,)),
        ],
        compiler_params=pltpu.CompilerParams(
            collective_id=0, has_side_effects=True, vmem_limit_bytes=63 * 1024 * 1024
        ),
    )(
        lengths,
        residual,
        norm_gain,
        expert_ids,
        gate_values,
        query_latent,
        query_rope,
        cache_latent,
        cache_rope,
        value_up,
        out_proj,
        w_gate,
        w_up,
        w_down,
    )


def local(
    query_latent,
    query_rope,
    cache_latent,
    cache_rope,
    lengths,
    value_up,
    out_proj,
    residual,
    norm_gain,
    expert_ids,
    gate_values,
    w_gate,
    w_up,
    w_down,
):
    return layer(
        lengths,
        residual,
        norm_gain[None, :],
        expert_ids,
        gate_values,
        query_latent,
        jnp.swapaxes(query_rope, 1, 2),
        cache_latent,
        cache_rope,
        value_up,
        out_proj,
        w_gate[0],
        w_up[0],
        w_down[0],
    )


def solution(mesh):
    finer = Mesh(
        mesh.devices.reshape(mesh.shape["group"], 4, 2, 4, 2),
        ("group", "dev_0", "dev_1", "dev_2", "dev_3"),
    )
    return jax.shard_map(
        local,
        mesh=finer,
        in_specs=(
            P(GROUP_DEV, None, None),
            P(GROUP_DEV, None, None),
            P(GROUP_DEV, None, None),
            P(GROUP_DEV, None, None),
            P(GROUP_DEV),
            P(DEV, None, None),
            P(DEV, None),
            P(GROUP_DEV, None),
            P(),
            P(GROUP_DEV, None),
            P(GROUP_DEV, None),
            P(DEV, None, "group"),
            P(DEV, None, "group"),
            P(DEV, "group", None),
        ),
        out_specs=P(GROUP_DEV, None),
        check_vma=False,
    )
```

```python
import functools

import jax
import jax.numpy as jnp
from jax import lax
from jax.experimental import pallas as pl
from jax.experimental.pallas import tpu as pltpu
from jax.sharding import Mesh
from jax.sharding import PartitionSpec as P

DEV = ("dev_0", "dev_1", "dev_2", "dev_3")
GROUP_DEV = ("group", "dev_0", "dev_1", "dev_2", "dev_3")
MESH = pl.DeviceIdType.MESH


softmax_scale = 192.0 ** (-0.5)


HALF = 3584
UNIT = 256
ATTN_COLS = (((0, 896), (896, 896)), ((1792, 896), (2688, 896)))
ATTN_ORDERS = (("z", "y"), ("y", "z"))
GATHER_COLS = (((0, 640), (640, 640)), ((1280, 640), (1920, 640)), ((2560, 640), (3200, 512)))
MIX_COLS = (((0, 640), (640, 512)), ((1152, 640), (1792, 640)), ((2432, 640), (3072, 512)))
ORDERS = (("z", "y", "x"), ("y", "x", "z"), ("x", "z", "y"))


def layer_kernel(
    lengths_ref,
    residual_ref,
    gain_ref,
    ids_ref,
    gate_values_ref,
    query_hbm,
    query_rope_hbm,
    cache_hbm,
    cache_rope_hbm,
    value_hbm,
    proj_hbm,
    gate_hbm,
    up_hbm,
    down_hbm,
    out_ref,
    query,
    query_rope,
    cache,
    cache_rope,
    scores,
    probs,
    latent_all,
    latent_out,
    latent_in,
    value_up,
    even_part,
    odd_part,
    even_values,
    odd_values,
    proj,
    w_gate,
    w_up,
    w_down,
    values,
    attn_sum,
    attn_land0a,
    attn_land0b,
    attn_land1,
    attn_land2,
    residual_out,
    residual_in,
    gates_out,
    gates_in,
    square_out,
    square_in,
    stream,
    swap_out,
    swap_in,
    rows,
    gate_acc,
    up_acc,
    active,
    mix_sum,
    mix_land0,
    mix_land1,
    mix_land2,
    cache_sem,
    load_sem,
    latent_send,
    latent_recv,
    send_sem,
    recv_sem,
):
    group = lax.axis_index("group")
    x_lo = lax.axis_index("dev_1")
    core = lax.axis_index("dev_3")
    pos = {"z": lax.axis_index("dev_0"), "y": lax.axis_index("dev_2"), "x": 2 * group + x_lo}
    other = 1 - core
    first_core = core == 0

    def above(dim):
        return lax.rem(pos[dim] + 1, 4)

    def below(dim):
        return lax.rem(pos[dim] + 3, 4)

    def across(dim):
        return lax.rem(pos[dim] + 2, 4)

    def device(dim, place):
        if dim == "z":
            return {"dev_0": place}
        if dim == "y":
            return {"dev_2": place}
        return {"group": lax.div(place, 2), "dev_1": lax.rem(place, 2)}

    partner = {"dev_3": other}
    x_pair = {"dev_1": 1 - x_lo}
    sent = []

    def send(src, dst, to):
        number = len(sent)
        copy = pltpu.make_async_remote_copy(
            src_ref=src,
            dst_ref=dst,
            send_sem=send_sem.at[number],
            recv_sem=recv_sem.at[number],
            device_id=to,
            device_id_type=MESH,
        )
        copy.start()
        sent.append(copy)
        return copy

    def load(number, src, dst):
        copy = pltpu.make_async_copy(src, dst, load_sem.at[number])
        copy.start()
        return copy

    def load_cache(token):
        slot = token % 2
        copy = pltpu.make_async_copy(cache_hbm.at[token], cache.at[slot], cache_sem.at[slot])
        copy.start()
        return copy

    query_load = load(4, query_hbm, query)
    query_rope_load = load(5, query_rope_hbm, query_rope)
    cache_loads = [load_cache(0)]
    cache_rope_load = load(6, cache_rope_hbm, cache_rope)
    cache_loads.append(load_cache(1))

    place = ((pos["z"] * 2 + x_lo) * 4 + pos["y"]) * 2 + core

    def peer(step):
        number = lax.rem(place + step, 64)
        return number, {
            "dev_0": lax.div(number, 16),
            "dev_1": lax.rem(lax.div(number, 8), 2),
            "dev_2": lax.rem(lax.div(number, 2), 4),
            "dev_3": lax.rem(number, 2),
        }

    barrier = pltpu.get_barrier_semaphore()

    def greet(step, carry):
        pl.semaphore_signal(barrier, inc=1, device_id=peer(step)[1], device_id_type=MESH)
        return carry

    lax.fori_loop(1, 64, greet, 0)
    for far_x in (lax.rem(pos["x"] + 3 + 2 * x_lo, 4), across("x")):
        pl.semaphore_signal(barrier, inc=1, device_id=device("x", far_x), device_id_type=MESH)

    own_half = pl.ds(pl.multiple_of(core * HALF, 128), HALF)
    other_half = pl.ds(pl.multiple_of(other * HALF, 128), HALF)
    own_rows = pl.ds(pl.multiple_of(core * 256, 256), 256)
    residual_out[...] = residual_ref[:, other_half]
    lane = lax.broadcasted_iota(jnp.int32, (4, 128), 1)
    gates = jnp.zeros((4, 128), jnp.float32)
    for choice in range(8):
        named = lax.rem(lane, 32) == ids_ref[:, choice : choice + 1]
        gates = gates + jnp.where(named, gate_values_ref[:, choice : choice + 1], 0.0)
    gates_out[...] = gates

    def eight_rows(mine, theirs):
        return jnp.concatenate(
            [jnp.where(first_core, mine, theirs), jnp.where(first_core, theirs, mine)], axis=0
        )

    def scatter_pair(pair):
        latent_out[pair] = latent_all[...].astype(jnp.bfloat16)

        def scatter(step, carry):
            number, to = peer(lax.rem(step * 19, 64))
            pltpu.make_async_remote_copy(
                src_ref=latent_out.at[pair, number],
                dst_ref=latent_in.at[pair, place],
                send_sem=latent_send.at[pair],
                recv_sem=latent_recv.at[pair],
                device_id=to,
                device_id_type=MESH,
            ).start()
            return carry

        lax.fori_loop(1, 64, scatter, 0)
        latent_in[pair, place] = latent_out[pair, place]

    def latent_copies(pair):
        return pltpu.make_async_remote_copy(
            src_ref=latent_out.at[pair, pl.ds(0, 63)],
            dst_ref=latent_in.at[pair, pl.ds(0, 63)],
            send_sem=latent_send.at[pair],
            recv_sem=latent_recv.at[pair],
            device_id=partner,
            device_id_type=MESH,
        )

    query_load.wait()
    query_rope_load.wait()
    loads = {}
    for token in range(4):
        slot = token % 2
        cache_loads[token].wait()
        if token == 0:
            cache_rope_load.wait()
            loads["value"] = load(7, value_hbm, value_up)
            loads["proj"] = load(0, proj_hbm.at[:, own_half], proj.at[own_rows])
        length = lengths_ref[token]
        peak = jnp.full((128, 1), -jnp.inf, jnp.float32)
        for start in range(0, 2048, 512):
            cols = pl.ds(start, 512)
            part = lax.dot_general(
                query[token],
                cache[slot, cols, :],
                (((1,), (1,)), ((), ())),
                preferred_element_type=jnp.float32,
            ) + lax.dot_general(
                query_rope[token],
                cache_rope[token, :, cols],
                (((0,), (0,)), ((), ())),
                preferred_element_type=jnp.float32,
            )
            slots = lax.broadcasted_iota(jnp.int32, part.shape, 1) + start
            part = jnp.where(slots < length, part, -jnp.inf)
            scores[:, cols] = part
            peak = jnp.maximum(peak, jnp.max(part, axis=1, keepdims=True))
        total = jnp.zeros((128, 1), jnp.float32)
        for start in range(0, 2048, 512):
            cols = pl.ds(start, 512)
            weights = jnp.exp((scores[:, cols] - peak) * softmax_scale)
            total = total + jnp.sum(weights, axis=1, keepdims=True)
            probs[:, cols] = weights.astype(jnp.bfloat16)
        mixed = jnp.dot(probs[...], cache[slot], preferred_element_type=jnp.float32) / total
        latent_all[:, 2 * slot : 2 * slot + 2, :] = mixed.reshape(64, 2, 512)
        if token + 2 < 4:
            cache_loads.append(load_cache(token + 2))
        if token == 1:
            pl.semaphore_wait(barrier, 65)
            handed = {
                "residual": send(residual_out, residual_in, partner),
                "gates": send(gates_out, gates_in, partner),
                "proj": send(proj_hbm.at[:, other_half], proj.at[own_rows], partner),
            }
            loads["gate"] = load(1, gate_hbm, w_gate)
        elif token == 2:
            loads["up"] = load(2, up_hbm, w_up)
            loads["down"] = load(3, down_hbm.at[:, own_half], w_down.at[own_rows])
            handed["down"] = send(down_hbm.at[:, other_half], w_down.at[own_rows], partner)
        if token % 2 == 1:
            scatter_pair(token // 2)

    loads["value"].wait()
    for pair in range(2):
        latent_copies(pair).wait_recv()
        latents = latent_in[pair].reshape(256, 512)
        even_part[...] = jnp.dot(latents, value_up[0], preferred_element_type=jnp.float32)
        odd_part[...] = jnp.dot(latents, value_up[1], preferred_element_type=jnp.float32)
        for part, kept in ((even_part, even_values), (odd_part, odd_values)):
            first = 0 if part is even_part else 1
            heads = part[pl.ds(first, 128, stride=2), :].reshape(32, 2, 2, 128)
            for owner in range(2):
                at = 4 * owner + 2 * pair
                kept[:, at : at + 2, :] = heads[:, owner]
    values[core] = jnp.concatenate(
        [even_values[...].reshape(256, 128), odd_values[...].reshape(256, 128)], axis=1
    ).astype(jnp.bfloat16)

    def ring_start(dim, block, land, cols, part):
        first, second = cols
        up, down = device(dim, above(dim)), device(dim, below(dim))
        if part == 0:
            return (
                send(block(across(dim), first), land(0, first), up),
                send(block(below(dim), first), land(1, first), down),
            )
        return (
            send(block(across(dim), second), land(2, second), down),
            send(block(above(dim), second), land(3, second), up),
        )

    def add_into(target, *terms):
        total = target[...].astype(jnp.float32)
        for term in terms:
            total = total + term[...].astype(jnp.float32)
        return total

    def ring_relay(dim, block, land, cols, started):
        first, second = cols
        up, down = device(dim, above(dim)), device(dim, below(dim))
        started[0][0].wait_recv()
        target = block(above(dim), first)
        target[...] = add_into(target, land(0, first)).astype(jnp.bfloat16)
        upward = send(target, land(4, first), up)
        started[1][0].wait_recv()
        target = block(below(dim), second)
        target[...] = add_into(target, land(2, second)).astype(jnp.bfloat16)
        downward = send(target, land(5, second), down)
        return upward, downward

    def ring_finish(dim, block, land, cols, started, relayed, store):
        first, second = cols
        started[0][1].wait_recv()
        relayed[0].wait_recv()
        store(first, add_into(block(pos[dim], first), land(1, first), land(4, first)))
        started[1][1].wait_recv()
        relayed[1].wait_recv()
        store(second, add_into(block(pos[dim], second), land(3, second), land(5, second)))

    def direct_start(dim, block, land, cols):
        return [
            send(block(where(dim), cols), land(slot, cols), device(dim, where(dim)))
            for slot, where in enumerate((above, below, across))
        ]

    def direct_finish(dim, block, land, cols, started, store):
        for copy in started:
            copy.wait_recv()
        store(cols, add_into(block(pos[dim], cols), *(land(slot, cols) for slot in range(3))))

    def whole_cols(cols):
        return cols[0][0], cols[0][1] + cols[1][1]

    def span(cols):
        return pl.ds(cols[0], cols[1])

    handed["values"] = send(values.at[core], values.at[core], partner)

    def attn_block(rotation, phase):
        dims = ATTN_ORDERS[rotation]

        def block(place, cols):
            at = {}
            for earlier in dims[:phase]:
                at[earlier] = pos[earlier]
            at[dims[phase]] = place
            return attn_sum.at[
                at.get("z", slice(None)), slice(None), at.get("y", slice(None)), slice(None), span(cols)
            ]

        return block

    def attn_land(rotation, phase):
        if phase == 0:
            land = (attn_land0a, attn_land0b)[rotation]
            return lambda slot, cols: land.at[
                slot, slice(None), slice(None), slice(None), pl.ds(0, cols[1])
            ]
        return lambda slot, cols: attn_land1.at[
            rotation, slot, slice(None), slice(None), pl.ds(0, cols[1])
        ]

    started = {}
    loads["proj"].wait()
    handed["proj"].wait_recv()
    handed["values"].wait_recv()
    for rotation in range(2):
        for part in range(2):
            cols = ATTN_COLS[rotation][part]
            for start in range(cols[0], cols[0] + cols[1], UNIT):
                width = min(UNIT, cols[0] + cols[1] - start)
                piece = pl.ds(start, width)
                share = jnp.dot(
                    values[0], proj[0:256, piece], preferred_element_type=jnp.float32
                ) + jnp.dot(values[1], proj[256:512, piece], preferred_element_type=jnp.float32)
                attn_sum[:, :, :, :, piece] = share.reshape(4, 2, 4, 8, width).astype(jnp.bfloat16)
            started[rotation, part] = ring_start(
                ATTN_ORDERS[rotation][0],
                attn_block(rotation, 0),
                attn_land(rotation, 0),
                ATTN_COLS[rotation],
                part,
            )
    relayed = {}
    for rotation in range(2):
        relayed[rotation] = ring_relay(
            ATTN_ORDERS[rotation][0],
            attn_block(rotation, 0),
            attn_land(rotation, 0),
            ATTN_COLS[rotation],
            (started[rotation, 0], started[rotation, 1]),
        )

    def keep_in(block, dim):
        def store(cols, total):
            block(pos[dim], cols)[...] = total.astype(jnp.bfloat16)

        return store

    for rotation in range(2):
        dim, next_dim = ATTN_ORDERS[rotation]
        block = attn_block(rotation, 0)
        ring_finish(
            dim,
            block,
            attn_land(rotation, 0),
            ATTN_COLS[rotation],
            (started[rotation, 0], started[rotation, 1]),
            relayed[rotation],
            keep_in(block, dim),
        )
        started[rotation] = direct_start(
            next_dim, attn_block(rotation, 1), attn_land(rotation, 1), whole_cols(ATTN_COLS[rotation])
        )
    paired = {}
    for rotation in range(2):
        dim = ATTN_ORDERS[rotation][1]
        block = attn_block(rotation, 1)
        cols = whole_cols(ATTN_COLS[rotation])
        direct_finish(
            dim, block, attn_land(rotation, 1), cols, started[rotation], keep_in(block, dim)
        )
        paired[rotation] = send(
            attn_sum.at[pos["z"], 1 - x_lo, pos["y"], slice(None), span(cols)],
            attn_land2.at[slice(None), span(cols)],
            x_pair,
        )
    handed["residual"].wait_recv()
    handed["gates"].wait_recv()
    for rotation in range(2):
        paired[rotation].wait_recv()
    residual = eight_rows(
        residual_ref[:, own_half].astype(jnp.float32), residual_in[...].astype(jnp.float32)
    )
    stream[...] = (
        residual
        + attn_sum[pos["z"], x_lo, pos["y"]].astype(jnp.float32)
        + attn_land2[...].astype(jnp.float32)
    )
    square = jnp.sum(stream[...] * stream[...], axis=1, keepdims=True)
    square_out[...] = jnp.broadcast_to(square, (8, 128))
    squared = send(square_out, square_in, partner)
    dense = eight_rows(gates_out[...], gates_in[...])
    coarse = dense.astype(jnp.bfloat16).astype(jnp.float32)
    lane = lax.broadcasted_iota(jnp.int32, dense.shape, 1)
    packed = jnp.where(lane < 32, coarse, jnp.where(lane < 64, dense - coarse, 0.0))
    mine = (core, pos["x"], pos["y"], pos["z"])
    rows[mine + (slice(None), pl.ds(HALF, 128))] = packed.astype(jnp.bfloat16)
    squared.wait_recv()
    total = square_out[:, 0:1] + square_in[:, 0:1]
    scale = lax.rsqrt(total / (2 * HALF) + 1e-06)
    rows[mine + (slice(None), pl.ds(0, HALF))] = (
        stream[...] * scale * gain_ref[:, own_half]
    ).astype(jnp.bfloat16)

    def row_block(at, cols):
        return rows.at[
            core,
            at.get("x", slice(None)),
            at.get("y", slice(None)),
            at.get("z", slice(None)),
            slice(None),
            span(cols),
        ]

    shared = []
    opened = {}
    for rotation in range(3):
        dim = ORDERS[rotation][0]
        own = row_block(pos, whole_cols(GATHER_COLS[rotation]))
        opened[rotation] = [
            send(own, own, device(dim, where(dim))) for where in (above, below, across)
        ]
    for rotation in range(3):
        for copy in opened[rotation]:
            copy.wait_recv()
    def gather_dims(rotation):
        first, second = GATHER_COLS[rotation]
        return ORDERS[rotation], first, second

    def open_ring(dim, at, first, second):
        up, down = device(dim, above(dim)), device(dim, below(dim))
        one, two = row_block(at, first), row_block(at, second)
        return (
            send(one, one, up),
            send(two, two, down),
            send(two, two, up),
            send(one, one, down),
        )

    def forward(dim, at, first, second, begun):
        begun[0].wait_recv()
        one = row_block({**at, dim: below(dim)}, first)
        upward = send(one, one, device(dim, above(dim)))
        begun[1].wait_recv()
        two = row_block({**at, dim: above(dim)}, second)
        return upward, send(two, two, device(dim, below(dim)))

    def hand_over(rotation, at):
        piece = row_block(at, whole_cols(GATHER_COLS[rotation]))
        return send(piece, piece, partner)

    middle, outer, passed, shared = {}, {}, {}, {}
    for rotation in range(3):
        (a, b, c), first, second = gather_dims(rotation)
        middle[rotation] = open_ring(b, {b: pos[b], c: pos[c]}, first, second)
    for rotation in range(3):
        (a, b, c), first, second = gather_dims(rotation)
        at = {b: pos[b], c: pos[c]}
        outer[rotation, "own"] = open_ring(c, at, first, second)
    for rotation in range(3):
        (a, b, c), first, second = gather_dims(rotation)
        passed[rotation] = forward(b, {c: pos[c]}, first, second, middle[rotation])
    for rotation in range(3):
        (a, b, c), first, second = gather_dims(rotation)
        middle[rotation][2].wait_recv()
        middle[rotation][3].wait_recv()
        for where in (below, above):
            outer[rotation, where] = open_ring(c, {b: where(b), c: pos[c]}, first, second)
    onward = {}
    for rotation in range(3):
        (a, b, c), first, second = gather_dims(rotation)
        onward[rotation, "own"] = forward(c, {b: pos[b]}, first, second, outer[rotation, "own"])
    for rotation in range(3):
        (a, b, c), first, second = gather_dims(rotation)
        passed[rotation][0].wait_recv()
        passed[rotation][1].wait_recv()
        outer[rotation, across] = open_ring(c, {b: across(b), c: pos[c]}, first, second)
        shared[rotation, "own"] = [hand_over(rotation, {c: pos[c]})]
    loads["gate"].wait()
    loads["up"].wait()

    def acc_rows(acc, at):
        return acc.at[at.get("x", slice(None)), at.get("y", slice(None)), at.get("z", slice(None))]

    def multiply(half, rotation, at):
        start = GATHER_COLS[rotation][0][0]
        depth = min(whole_cols(GATHER_COLS[rotation])[1], HALF - start)
        index = (at.get("x", slice(None)), at.get("y", slice(None)), at.get("z", slice(None)))
        lhs = rows[(half,) + index + (slice(None), pl.ds(start, depth))].reshape(128, depth)
        weight_rows = pl.ds(pl.multiple_of(half * HALF + start, 128), depth)
        for acc, weight in ((gate_acc, w_gate), (up_acc, w_up)):
            part = jnp.dot(
                lhs, weight[weight_rows, :], preferred_element_type=jnp.float32
            ).reshape(4, 4, 8, 256)
            acc_rows(acc, at)[...] += part

    gate_acc[...] = jnp.zeros_like(gate_acc)
    up_acc[...] = jnp.zeros_like(up_acc)
    for rotation in range(3):
        c = ORDERS[rotation][2]
        multiply(core, rotation, {c: pos[c]})
    for name, where in (("below", below), ("above", above), ("across", across)):
        for rotation in range(3):
            (a, b, c), first, second = gather_dims(rotation)
            onward[rotation, name] = forward(c, {b: where(b)}, first, second, outer[rotation, where])
    for rotation in range(3):
        c = ORDERS[rotation][2]
        shared[rotation, "own"][0].wait_recv()
        multiply(other, rotation, {c: pos[c]})
    for rotation in range(3):
        c = ORDERS[rotation][2]
        for key in ("own", below, above, across):
            outer[rotation, key][2].wait_recv()
            outer[rotation, key][3].wait_recv()
        for where in (below, above):
            shared[rotation, where] = [hand_over(rotation, {c: where(c)})]
    for where in (below, above):
        for rotation in range(3):
            c = ORDERS[rotation][2]
            multiply(core, rotation, {c: where(c)})
    for rotation in range(3):
        b, c = ORDERS[rotation][1:]
        shared[rotation, across] = []
        for name, there in (("own", None), ("below", below), ("above", above), ("across", across)):
            for copy in onward[rotation, name]:
                copy.wait_recv()
            at = {c: across(c), b: pos[b] if there is None else there(b)}
            shared[rotation, across].append(hand_over(rotation, at))
    for where in (below, above):
        for rotation in range(3):
            c = ORDERS[rotation][2]
            shared[rotation, where][0].wait_recv()
            multiply(other, rotation, {c: where(c)})
    for rotation in range(3):
        c = ORDERS[rotation][2]
        multiply(core, rotation, {c: across(c)})
    for rotation in range(3):
        c = ORDERS[rotation][2]
        for copy in shared[rotation, across]:
            copy.wait_recv()
        multiply(other, rotation, {c: across(c)})

    expert = (pos["z"] * 2 + x_lo) * 4 + pos["y"]
    parts = rows[0, :, :, :, :, HALF : HALF + 128].astype(jnp.float32).reshape(512, 128)
    lane = lax.broadcasted_iota(jnp.int32, parts.shape, 1)
    picked = jnp.where((lane == expert) | (lane == expert + 32), parts, 0.0)
    row_gate = jnp.sum(picked, axis=1, keepdims=True)
    gate_part = gate_acc[...].reshape(512, 256)
    active[core] = (gate_part * jax.nn.sigmoid(gate_part) * up_acc[...].reshape(512, 256) * row_gate).astype(
        jnp.bfloat16
    )

    handed["active"] = send(active.at[core], active.at[core], partner)
    loads["down"].wait()
    handed["down"].wait_recv()
    handed["active"].wait_recv()

    def mix_block(rotation, phase):
        dims = ORDERS[rotation][::-1]

        def block(place, cols):
            at = {}
            for earlier in dims[:phase]:
                at[earlier] = pos[earlier]
            at[dims[phase]] = place
            return mix_sum.at[
                at.get("x", slice(None)),
                at.get("y", slice(None)),
                at.get("z", slice(None)),
                slice(None),
                span(cols),
            ]

        return block

    def mix_land(rotation, phase):
        land = (mix_land0, mix_land1, mix_land2)[phase]

        def place(slot, cols):
            return land.at[
                (rotation, slot) + (slice(None),) * (3 - phase) + (pl.ds(0, cols[1]),)
            ]

        return place

    started, relayed = {}, {}

    def mix_relay(rotation, phase):
        relayed[rotation] = ring_relay(
            ORDERS[rotation][2 - phase],
            mix_block(rotation, phase),
            mix_land(rotation, phase),
            MIX_COLS[rotation],
            (started[rotation, 0], started[rotation, 1]),
        )

    for rotation in range(3):
        for part in range(2):
            cols = MIX_COLS[rotation][part]
            for start in range(cols[0], cols[0] + cols[1], UNIT):
                width = min(UNIT, cols[0] + cols[1] - start)
                piece = pl.ds(start, width)
                share = jnp.dot(
                    active[0], w_down[0:256, piece], preferred_element_type=jnp.float32
                ) + jnp.dot(active[1], w_down[256:512, piece], preferred_element_type=jnp.float32)
                mix_sum[:, :, :, :, piece] = share.reshape(4, 4, 4, 8, width).astype(jnp.bfloat16)
            started[rotation, part] = ring_start(
                ORDERS[rotation][2], mix_block(rotation, 0), mix_land(rotation, 0), MIX_COLS[rotation], part
            )
    for rotation in range(3):
        mix_relay(rotation, 0)
    for phase in range(2):
        if phase == 1:
            for rotation in range(3):
                mix_relay(rotation, 1)
        for rotation in range(3):
            dim = ORDERS[rotation][2 - phase]
            block = mix_block(rotation, phase)
            ring_finish(
                dim,
                block,
                mix_land(rotation, phase),
                MIX_COLS[rotation],
                (started[rotation, 0], started[rotation, 1]),
                relayed[rotation],
                keep_in(block, dim),
            )
            if phase == 0:
                for part in range(2):
                    started[rotation, part] = ring_start(
                        ORDERS[rotation][1],
                        mix_block(rotation, 1),
                        mix_land(rotation, 1),
                        MIX_COLS[rotation],
                        part,
                    )
            else:
                started[rotation] = direct_start(
                    ORDERS[rotation][0],
                    mix_block(rotation, 2),
                    mix_land(rotation, 2),
                    whole_cols(MIX_COLS[rotation]),
                )

    def add_to_stream(cols, total):
        stream[:, span(cols)] += total

    for rotation in range(3):
        direct_finish(
            ORDERS[rotation][0],
            mix_block(rotation, 2),
            mix_land(rotation, 2),
            whole_cols(MIX_COLS[rotation]),
            started[rotation],
            add_to_stream,
        )
    top, bottom = stream[0:4, :], stream[4:8, :]
    swap_out[...] = jnp.where(first_core, bottom, top)
    swapped = send(swap_out, swap_in, partner)
    mine = jnp.where(first_core, top, bottom)
    swapped.wait_recv()
    theirs = swap_in[...]
    out_ref[:, 0:HALF] = jnp.where(first_core, mine, theirs).astype(jnp.bfloat16)
    out_ref[:, HALF : 2 * HALF] = jnp.where(first_core, theirs, mine).astype(jnp.bfloat16)
    for copy in sent:
        copy.wait_send()
    for pair in range(2):
        latent_copies(pair).wait_send()


def layer(
    lengths,
    residual,
    norm_gain,
    expert_ids,
    gate_values,
    query_latent,
    query_rope,
    cache_latent,
    cache_rope,
    value_up,
    out_proj,
    w_gate,
    w_up,
    w_down,
):
    bf16, f32 = jnp.bfloat16, jnp.float32
    vmem = pl.BlockSpec(memory_space=pltpu.VMEM)
    hbm = pl.BlockSpec(memory_space=pl.ANY)
    return pl.pallas_call(
        layer_kernel,
        out_shape=jax.ShapeDtypeStruct((4, 2 * HALF), bf16),
        in_specs=[pl.BlockSpec(memory_space=pltpu.SMEM)] + [vmem] * 4 + [hbm] * 9,
        out_specs=vmem,
        scratch_shapes=[
            pltpu.VMEM(query_latent.shape, bf16),
            pltpu.VMEM(query_rope.shape, bf16),
            pltpu.VMEM((2, 2048, 512), bf16),
            pltpu.VMEM(cache_rope.shape, bf16),
            pltpu.VMEM((128, 2048), f32),
            pltpu.VMEM((128, 2048), bf16),
            pltpu.VMEM((64, 4, 512), f32),
            pltpu.VMEM((2, 64, 4, 512), bf16),
            pltpu.VMEM((2, 64, 4, 512), bf16),
            pltpu.VMEM(value_up.shape, bf16),
            pltpu.VMEM((256, 128), f32),
            pltpu.VMEM((256, 128), f32),
            pltpu.VMEM((32, 8, 128), f32),
            pltpu.VMEM((32, 8, 128), f32),
            pltpu.VMEM((512, HALF), bf16),
            pltpu.VMEM(w_gate.shape, bf16),
            pltpu.VMEM(w_up.shape, bf16),
            pltpu.VMEM((512, HALF), bf16),
            pltpu.VMEM((2, 256, 256), bf16),
            pltpu.VMEM((4, 2, 4, 8, HALF), bf16),
            pltpu.VMEM((6, 2, 4, 8, 1024), bf16),
            pltpu.VMEM((6, 4, 2, 8, 1024), bf16),
            pltpu.VMEM((2, 3, 2, 8, 1792), bf16),
            pltpu.VMEM((8, HALF), bf16),
            pltpu.VMEM((4, HALF), bf16),
            pltpu.VMEM((4, HALF), bf16),
            pltpu.VMEM((4, 128), f32),
            pltpu.VMEM((4, 128), f32),
            pltpu.VMEM((8, 128), f32),
            pltpu.VMEM((8, 128), f32),
            pltpu.VMEM((8, HALF), f32),
            pltpu.VMEM((4, HALF), f32),
            pltpu.VMEM((4, HALF), f32),
            pltpu.VMEM((2, 4, 4, 4, 8, HALF + 128), bf16),
            pltpu.VMEM((4, 4, 4, 8, 256), f32),
            pltpu.VMEM((4, 4, 4, 8, 256), f32),
            pltpu.VMEM((2, 512, 256), bf16),
            pltpu.VMEM((4, 4, 4, 8, HALF), bf16),
            pltpu.VMEM((3, 6, 4, 4, 8, 768), bf16),
            pltpu.VMEM((3, 6, 4, 8, 768), bf16),
            pltpu.VMEM((3, 3, 8, 1280), bf16),
            pltpu.SemaphoreType.DMA((2,)),
            pltpu.SemaphoreType.DMA((8,)),
            pltpu.SemaphoreType.DMA((2,)),
            pltpu.SemaphoreType.DMA((2,)),
            pltpu.SemaphoreType.DMA((240,)),
            pltpu.SemaphoreType.DMA((240,)),
        ],
        compiler_params=pltpu.CompilerParams(
            collective_id=0, has_side_effects=True, vmem_limit_bytes=63 * 1024 * 1024
        ),
    )(
        lengths,
        residual,
        norm_gain,
        expert_ids,
        gate_values,
        query_latent,
        query_rope,
        cache_latent,
        cache_rope,
        value_up,
        out_proj,
        w_gate,
        w_up,
        w_down,
    )


def local(
    query_latent,
    query_rope,
    cache_latent,
    cache_rope,
    lengths,
    value_up,
    out_proj,
    residual,
    norm_gain,
    expert_ids,
    gate_values,
    w_gate,
    w_up,
    w_down,
):
    return layer(
        lengths,
        residual,
        norm_gain[None, :],
        expert_ids,
        gate_values,
        query_latent,
        jnp.swapaxes(query_rope, 1, 2),
        cache_latent,
        cache_rope,
        value_up,
        out_proj,
        w_gate[0],
        w_up[0],
        w_down[0],
    )


def solution(mesh):
    finer = Mesh(
        mesh.devices.reshape(mesh.shape["group"], 4, 2, 4, 2),
        ("group", "dev_0", "dev_1", "dev_2", "dev_3"),
    )
    return jax.shard_map(
        local,
        mesh=finer,
        in_specs=(
            P(GROUP_DEV, None, None),
            P(GROUP_DEV, None, None),
            P(GROUP_DEV, None, None),
            P(GROUP_DEV, None, None),
            P(GROUP_DEV),
            P(DEV, None, None),
            P(DEV, None),
            P(GROUP_DEV, None),
            P(),
            P(GROUP_DEV, None),
            P(GROUP_DEV, None),
            P(DEV, None, "group"),
            P(DEV, None, "group"),
            P(DEV, "group", None),
        ),
        out_specs=P(GROUP_DEV, None),
        check_vma=False,
    )
```

```python
import functools

import jax
import jax.numpy as jnp
from jax import lax
from jax.experimental import pallas as pl
from jax.experimental.pallas import tpu as pltpu
from jax.sharding import Mesh
from jax.sharding import PartitionSpec as P

DEV = ("dev_0", "dev_1", "dev_2", "dev_3")
GROUP_DEV = ("group", "dev_0", "dev_1", "dev_2", "dev_3")
MESH = pl.DeviceIdType.MESH


softmax_scale = 192.0 ** (-0.5)


HALF = 3584
UNIT = 256
ATTN_COLS = (((0, 896), (896, 896)), ((1792, 896), (2688, 896)))
ATTN_ORDERS = (("z", "y"), ("y", "z"))
GATHER_COLS = (((0, 640), (640, 640)), ((1280, 640), (1920, 640)), ((2560, 640), (3200, 512)))
MIX_COLS = (((0, 640), (640, 512)), ((1152, 640), (1792, 640)), ((2432, 640), (3072, 512)))
ORDERS = (("z", "y", "x"), ("y", "x", "z"), ("x", "z", "y"))


def layer_kernel(
    lengths_ref,
    residual_ref,
    gain_ref,
    ids_ref,
    gate_values_ref,
    query_hbm,
    query_rope_hbm,
    cache_hbm,
    cache_rope_hbm,
    value_hbm,
    proj_hbm,
    gate_hbm,
    up_hbm,
    down_hbm,
    out_ref,
    query,
    query_rope,
    cache,
    cache_rope,
    scores,
    probs,
    latent_all,
    latent_out,
    latent_in,
    value_up,
    even_part,
    odd_part,
    even_values,
    odd_values,
    proj,
    w_gate,
    w_up,
    w_down,
    values,
    attn_sum,
    attn_land0a,
    attn_land0b,
    attn_land1,
    attn_land2,
    residual_out,
    residual_in,
    gates_out,
    gates_in,
    square_out,
    square_in,
    stream,
    swap_out,
    swap_in,
    rows,
    gate_acc,
    up_acc,
    active,
    mix_sum,
    mix_land0,
    mix_land1,
    mix_land2,
    cache_sem,
    load_sem,
    latent_send,
    latent_recv,
    send_sem,
    recv_sem,
):
    group = lax.axis_index("group")
    x_lo = lax.axis_index("dev_1")
    core = lax.axis_index("dev_3")
    pos = {"z": lax.axis_index("dev_0"), "y": lax.axis_index("dev_2"), "x": 2 * group + x_lo}
    other = 1 - core
    first_core = core == 0

    def above(dim):
        return lax.rem(pos[dim] + 1, 4)

    def below(dim):
        return lax.rem(pos[dim] + 3, 4)

    def across(dim):
        return lax.rem(pos[dim] + 2, 4)

    def device(dim, place):
        if dim == "z":
            return {"dev_0": place}
        if dim == "y":
            return {"dev_2": place}
        return {"group": lax.div(place, 2), "dev_1": lax.rem(place, 2)}

    partner = {"dev_3": other}
    x_pair = {"dev_1": 1 - x_lo}
    sent = []

    def send(src, dst, to):
        number = len(sent)
        copy = pltpu.make_async_remote_copy(
            src_ref=src,
            dst_ref=dst,
            send_sem=send_sem.at[number],
            recv_sem=recv_sem.at[number],
            device_id=to,
            device_id_type=MESH,
        )
        copy.start()
        sent.append(copy)
        return copy

    def load(number, src, dst):
        copy = pltpu.make_async_copy(src, dst, load_sem.at[number])
        copy.start()
        return copy

    def load_cache(token):
        slot = token % 2
        copy = pltpu.make_async_copy(cache_hbm.at[token], cache.at[slot], cache_sem.at[slot])
        copy.start()
        return copy

    query_load = load(4, query_hbm, query)
    query_rope_load = load(5, query_rope_hbm, query_rope)
    cache_loads = [load_cache(0)]
    cache_rope_load = load(6, cache_rope_hbm, cache_rope)
    cache_loads.append(load_cache(1))

    place = ((pos["z"] * 2 + x_lo) * 4 + pos["y"]) * 2 + core

    def peer(step):
        number = lax.rem(place + step, 64)
        return number, {
            "dev_0": lax.div(number, 16),
            "dev_1": lax.rem(lax.div(number, 8), 2),
            "dev_2": lax.rem(lax.div(number, 2), 4),
            "dev_3": lax.rem(number, 2),
        }

    barrier = pltpu.get_barrier_semaphore()

    def greet(step, carry):
        pl.semaphore_signal(barrier, inc=1, device_id=peer(step)[1], device_id_type=MESH)
        return carry

    lax.fori_loop(1, 64, greet, 0)
    for far_x in (lax.rem(pos["x"] + 3 + 2 * x_lo, 4), across("x")):
        pl.semaphore_signal(barrier, inc=1, device_id=device("x", far_x), device_id_type=MESH)

    own_half = pl.ds(pl.multiple_of(core * HALF, 128), HALF)
    other_half = pl.ds(pl.multiple_of(other * HALF, 128), HALF)
    own_rows = pl.ds(pl.multiple_of(core * 256, 256), 256)
    residual_out[...] = residual_ref[:, other_half]
    lane = lax.broadcasted_iota(jnp.int32, (4, 128), 1)
    gates = jnp.zeros((4, 128), jnp.float32)
    for choice in range(8):
        named = lax.rem(lane, 32) == ids_ref[:, choice : choice + 1]
        gates = gates + jnp.where(named, gate_values_ref[:, choice : choice + 1], 0.0)
    gates_out[...] = gates

    def eight_rows(mine, theirs):
        return jnp.concatenate(
            [jnp.where(first_core, mine, theirs), jnp.where(first_core, theirs, mine)], axis=0
        )

    def scatter_pair(pair):
        latent_out[pair] = latent_all[...].astype(jnp.bfloat16)

        def scatter(step, carry):
            number, to = peer(lax.rem(step * 19, 64))
            pltpu.make_async_remote_copy(
                src_ref=latent_out.at[pair, number],
                dst_ref=latent_in.at[pair, place],
                send_sem=latent_send.at[pair],
                recv_sem=latent_recv.at[pair],
                device_id=to,
                device_id_type=MESH,
            ).start()
            return carry

        lax.fori_loop(1, 64, scatter, 0)
        latent_in[pair, place] = latent_out[pair, place]

    def latent_copies(pair):
        return pltpu.make_async_remote_copy(
            src_ref=latent_out.at[pair, pl.ds(0, 63)],
            dst_ref=latent_in.at[pair, pl.ds(0, 63)],
            send_sem=latent_send.at[pair],
            recv_sem=latent_recv.at[pair],
            device_id=partner,
            device_id_type=MESH,
        )

    query_load.wait()
    query_rope_load.wait()
    loads = {}
    for token in range(4):
        slot = token % 2
        cache_loads[token].wait()
        if token == 0:
            cache_rope_load.wait()
            loads["value"] = load(7, value_hbm, value_up)
            loads["proj"] = load(0, proj_hbm.at[:, own_half], proj.at[own_rows])
        length = lengths_ref[token]
        peak = jnp.full((128, 1), -jnp.inf, jnp.float32)
        for start in range(0, 2048, 512):
            cols = pl.ds(start, 512)
            part = lax.dot_general(
                query[token],
                cache[slot, cols, :],
                (((1,), (1,)), ((), ())),
                preferred_element_type=jnp.float32,
            ) + lax.dot_general(
                query_rope[token],
                cache_rope[token, :, cols],
                (((0,), (0,)), ((), ())),
                preferred_element_type=jnp.float32,
            )
            slots = lax.broadcasted_iota(jnp.int32, part.shape, 1) + start
            part = jnp.where(slots < length, part, -jnp.inf)
            scores[:, cols] = part
            peak = jnp.maximum(peak, jnp.max(part, axis=1, keepdims=True))
        total = jnp.zeros((128, 1), jnp.float32)
        for start in range(0, 2048, 512):
            cols = pl.ds(start, 512)
            weights = jnp.exp((scores[:, cols] - peak) * softmax_scale)
            total = total + jnp.sum(weights, axis=1, keepdims=True)
            probs[:, cols] = weights.astype(jnp.bfloat16)
        mixed = jnp.dot(probs[...], cache[slot], preferred_element_type=jnp.float32) / total
        latent_all[:, 2 * slot : 2 * slot + 2, :] = mixed.reshape(64, 2, 512)
        if token + 2 < 4:
            cache_loads.append(load_cache(token + 2))
        if token == 1:
            pl.semaphore_wait(barrier, 65)
            handed = {
                "residual": send(residual_out, residual_in, partner),
                "gates": send(gates_out, gates_in, partner),
                "proj": send(proj_hbm.at[:, other_half], proj.at[own_rows], partner),
            }
            loads["gate"] = load(1, gate_hbm, w_gate)
        elif token == 2:
            loads["up"] = load(2, up_hbm, w_up)
            loads["down"] = load(3, down_hbm.at[:, own_half], w_down.at[own_rows])
            handed["down"] = send(down_hbm.at[:, other_half], w_down.at[own_rows], partner)
        if token % 2 == 1:
            scatter_pair(token // 2)

    loads["value"].wait()
    for pair in range(2):
        latent_copies(pair).wait_recv()
        latents = latent_in[pair].reshape(256, 512)
        even_part[...] = jnp.dot(latents, value_up[0], preferred_element_type=jnp.float32)
        odd_part[...] = jnp.dot(latents, value_up[1], preferred_element_type=jnp.float32)
        for part, kept in ((even_part, even_values), (odd_part, odd_values)):
            first = 0 if part is even_part else 1
            heads = part[pl.ds(first, 128, stride=2), :].reshape(32, 2, 2, 128)
            for owner in range(2):
                at = 4 * owner + 2 * pair
                kept[:, at : at + 2, :] = heads[:, owner]
    values[core] = jnp.concatenate(
        [even_values[...].reshape(256, 128), odd_values[...].reshape(256, 128)], axis=1
    ).astype(jnp.bfloat16)

    def ring_start(dim, block, land, cols, part):
        first, second = cols
        up, down = device(dim, above(dim)), device(dim, below(dim))
        if part == 0:
            return (
                send(block(across(dim), first), land(0, first), up),
                send(block(below(dim), first), land(1, first), down),
            )
        return (
            send(block(across(dim), second), land(2, second), down),
            send(block(above(dim), second), land(3, second), up),
        )

    def add_into(target, *terms):
        total = target[...].astype(jnp.float32)
        for term in terms:
            total = total + term[...].astype(jnp.float32)
        return total

    def ring_relay(dim, block, land, cols, started):
        first, second = cols
        up, down = device(dim, above(dim)), device(dim, below(dim))
        started[0][0].wait_recv()
        target = block(above(dim), first)
        target[...] = add_into(target, land(0, first)).astype(jnp.bfloat16)
        upward = send(target, land(4, first), up)
        started[1][0].wait_recv()
        target = block(below(dim), second)
        target[...] = add_into(target, land(2, second)).astype(jnp.bfloat16)
        downward = send(target, land(5, second), down)
        return upward, downward

    def ring_finish(dim, block, land, cols, started, relayed, store):
        first, second = cols
        started[0][1].wait_recv()
        relayed[0].wait_recv()
        store(first, add_into(block(pos[dim], first), land(1, first), land(4, first)))
        started[1][1].wait_recv()
        relayed[1].wait_recv()
        store(second, add_into(block(pos[dim], second), land(3, second), land(5, second)))

    def direct_start(dim, block, land, cols):
        return [
            send(block(where(dim), cols), land(slot, cols), device(dim, where(dim)))
            for slot, where in enumerate((above, below, across))
        ]

    def direct_finish(dim, block, land, cols, started, store):
        for copy in started:
            copy.wait_recv()
        store(cols, add_into(block(pos[dim], cols), *(land(slot, cols) for slot in range(3))))

    def whole_cols(cols):
        return cols[0][0], cols[0][1] + cols[1][1]

    def span(cols):
        return pl.ds(cols[0], cols[1])

    handed["values"] = send(values.at[core], values.at[core], partner)

    def attn_block(rotation, phase):
        dims = ATTN_ORDERS[rotation]

        def block(place, cols):
            at = {}
            for earlier in dims[:phase]:
                at[earlier] = pos[earlier]
            at[dims[phase]] = place
            return attn_sum.at[
                at.get("z", slice(None)), slice(None), at.get("y", slice(None)), slice(None), span(cols)
            ]

        return block

    def attn_land(rotation, phase):
        if phase == 0:
            land = (attn_land0a, attn_land0b)[rotation]
            return lambda slot, cols: land.at[
                slot, slice(None), slice(None), slice(None), pl.ds(0, cols[1])
            ]
        return lambda slot, cols: attn_land1.at[
            rotation, slot, slice(None), slice(None), pl.ds(0, cols[1])
        ]

    started = {}
    loads["proj"].wait()
    handed["proj"].wait_recv()
    handed["values"].wait_recv()
    for rotation in range(2):
        for part in range(2):
            cols = ATTN_COLS[rotation][part]
            for start in range(cols[0], cols[0] + cols[1], UNIT):
                width = min(UNIT, cols[0] + cols[1] - start)
                piece = pl.ds(start, width)
                share = jnp.dot(
                    values[0], proj[0:256, piece], preferred_element_type=jnp.float32
                ) + jnp.dot(values[1], proj[256:512, piece], preferred_element_type=jnp.float32)
                attn_sum[:, :, :, :, piece] = share.reshape(4, 2, 4, 8, width).astype(jnp.bfloat16)
            started[rotation, part] = ring_start(
                ATTN_ORDERS[rotation][0],
                attn_block(rotation, 0),
                attn_land(rotation, 0),
                ATTN_COLS[rotation],
                part,
            )
    relayed = {}
    for rotation in range(2):
        relayed[rotation] = ring_relay(
            ATTN_ORDERS[rotation][0],
            attn_block(rotation, 0),
            attn_land(rotation, 0),
            ATTN_COLS[rotation],
            (started[rotation, 0], started[rotation, 1]),
        )

    def keep_in(block, dim):
        def store(cols, total):
            block(pos[dim], cols)[...] = total.astype(jnp.bfloat16)

        return store

    for rotation in range(2):
        dim, next_dim = ATTN_ORDERS[rotation]
        block = attn_block(rotation, 0)
        ring_finish(
            dim,
            block,
            attn_land(rotation, 0),
            ATTN_COLS[rotation],
            (started[rotation, 0], started[rotation, 1]),
            relayed[rotation],
            keep_in(block, dim),
        )
        started[rotation] = direct_start(
            next_dim, attn_block(rotation, 1), attn_land(rotation, 1), whole_cols(ATTN_COLS[rotation])
        )
    paired = {}
    for rotation in range(2):
        dim = ATTN_ORDERS[rotation][1]
        block = attn_block(rotation, 1)
        cols = whole_cols(ATTN_COLS[rotation])
        direct_finish(
            dim, block, attn_land(rotation, 1), cols, started[rotation], keep_in(block, dim)
        )
        paired[rotation] = send(
            attn_sum.at[pos["z"], 1 - x_lo, pos["y"], slice(None), span(cols)],
            attn_land2.at[slice(None), span(cols)],
            x_pair,
        )
    handed["residual"].wait_recv()
    handed["gates"].wait_recv()
    for rotation in range(2):
        paired[rotation].wait_recv()
    residual = eight_rows(
        residual_ref[:, own_half].astype(jnp.float32), residual_in[...].astype(jnp.float32)
    )
    stream[...] = (
        residual
        + attn_sum[pos["z"], x_lo, pos["y"]].astype(jnp.float32)
        + attn_land2[...].astype(jnp.float32)
    )
    square = jnp.sum(stream[...] * stream[...], axis=1, keepdims=True)
    square_out[...] = jnp.broadcast_to(square, (8, 128))
    squared = send(square_out, square_in, partner)
    dense = eight_rows(gates_out[...], gates_in[...])
    coarse = dense.astype(jnp.bfloat16).astype(jnp.float32)
    lane = lax.broadcasted_iota(jnp.int32, dense.shape, 1)
    packed = jnp.where(lane < 32, coarse, jnp.where(lane < 64, dense - coarse, 0.0))
    mine = (core, pos["x"], pos["y"], pos["z"])
    rows[mine + (slice(None), pl.ds(HALF, 128))] = packed.astype(jnp.bfloat16)
    squared.wait_recv()
    total = square_out[:, 0:1] + square_in[:, 0:1]
    scale = lax.rsqrt(total / (2 * HALF) + 1e-06)
    rows[mine + (slice(None), pl.ds(0, HALF))] = (
        stream[...] * scale * gain_ref[:, own_half]
    ).astype(jnp.bfloat16)

    def row_block(at, cols):
        return rows.at[
            core,
            at.get("x", slice(None)),
            at.get("y", slice(None)),
            at.get("z", slice(None)),
            slice(None),
            span(cols),
        ]

    shared = []
    opened = {}
    for rotation in range(3):
        dim = ORDERS[rotation][0]
        own = row_block(pos, whole_cols(GATHER_COLS[rotation]))
        opened[rotation] = [
            send(own, own, device(dim, where(dim))) for where in (above, below, across)
        ]
    for rotation in range(3):
        for copy in opened[rotation]:
            copy.wait_recv()
    def gather_dims(rotation):
        first, second = GATHER_COLS[rotation]
        return ORDERS[rotation], first, second

    def open_ring(dim, at, first, second):
        up, down = device(dim, above(dim)), device(dim, below(dim))
        one, two = row_block(at, first), row_block(at, second)
        return (
            send(one, one, up),
            send(two, two, down),
            send(two, two, up),
            send(one, one, down),
        )

    def forward(dim, at, first, second, begun):
        begun[0].wait_recv()
        one = row_block({**at, dim: below(dim)}, first)
        upward = send(one, one, device(dim, above(dim)))
        begun[1].wait_recv()
        two = row_block({**at, dim: above(dim)}, second)
        return upward, send(two, two, device(dim, below(dim)))

    def hand_over(rotation, at):
        piece = row_block(at, whole_cols(GATHER_COLS[rotation]))
        return send(piece, piece, partner)

    middle, outer, passed, shared = {}, {}, {}, {}
    for rotation in range(3):
        (a, b, c), first, second = gather_dims(rotation)
        middle[rotation] = open_ring(b, {b: pos[b], c: pos[c]}, first, second)
    for rotation in range(3):
        (a, b, c), first, second = gather_dims(rotation)
        at = {b: pos[b], c: pos[c]}
        outer[rotation, "own"] = open_ring(c, at, first, second)
    for rotation in range(3):
        (a, b, c), first, second = gather_dims(rotation)
        passed[rotation] = forward(b, {c: pos[c]}, first, second, middle[rotation])
    for rotation in range(3):
        (a, b, c), first, second = gather_dims(rotation)
        middle[rotation][2].wait_recv()
        middle[rotation][3].wait_recv()
        for where in (below, above):
            outer[rotation, where] = open_ring(c, {b: where(b), c: pos[c]}, first, second)
    onward = {}
    for rotation in range(3):
        (a, b, c), first, second = gather_dims(rotation)
        onward[rotation, "own"] = forward(c, {b: pos[b]}, first, second, outer[rotation, "own"])
    for rotation in range(3):
        (a, b, c), first, second = gather_dims(rotation)
        passed[rotation][0].wait_recv()
        passed[rotation][1].wait_recv()
        outer[rotation, across] = open_ring(c, {b: across(b), c: pos[c]}, first, second)
        shared[rotation, "own"] = [hand_over(rotation, {c: pos[c]})]
    loads["gate"].wait()
    loads["up"].wait()

    def acc_rows(acc, at):
        return acc.at[at.get("x", slice(None)), at.get("y", slice(None)), at.get("z", slice(None))]

    def multiply(half, rotation, at):
        start = GATHER_COLS[rotation][0][0]
        depth = min(whole_cols(GATHER_COLS[rotation])[1], HALF - start)
        index = (at.get("x", slice(None)), at.get("y", slice(None)), at.get("z", slice(None)))
        lhs = rows[(half,) + index + (slice(None), pl.ds(start, depth))].reshape(128, depth)
        weight_rows = pl.ds(pl.multiple_of(half * HALF + start, 128), depth)
        for acc, weight in ((gate_acc, w_gate), (up_acc, w_up)):
            part = jnp.dot(
                lhs, weight[weight_rows, :], preferred_element_type=jnp.float32
            ).reshape(4, 4, 8, 256)
            acc_rows(acc, at)[...] += part

    gate_acc[...] = jnp.zeros_like(gate_acc)
    up_acc[...] = jnp.zeros_like(up_acc)
    for rotation in range(3):
        c = ORDERS[rotation][2]
        multiply(core, rotation, {c: pos[c]})
    for name, where in (("below", below), ("above", above), ("across", across)):
        for rotation in range(3):
            (a, b, c), first, second = gather_dims(rotation)
            onward[rotation, name] = forward(c, {b: where(b)}, first, second, outer[rotation, where])
    for rotation in range(3):
        c = ORDERS[rotation][2]
        shared[rotation, "own"][0].wait_recv()
        multiply(other, rotation, {c: pos[c]})
    for rotation in range(3):
        c = ORDERS[rotation][2]
        for key in ("own", below, above, across):
            outer[rotation, key][2].wait_recv()
            outer[rotation, key][3].wait_recv()
        for where in (below, above):
            shared[rotation, where] = [hand_over(rotation, {c: where(c)})]
    for where in (below, above):
        for rotation in range(3):
            c = ORDERS[rotation][2]
            multiply(core, rotation, {c: where(c)})
    for rotation in range(3):
        b, c = ORDERS[rotation][1:]
        shared[rotation, across] = []
        for name, there in (("own", None), ("below", below), ("above", above), ("across", across)):
            for copy in onward[rotation, name]:
                copy.wait_recv()
            at = {c: across(c), b: pos[b] if there is None else there(b)}
            shared[rotation, across].append(hand_over(rotation, at))
    for where in (below, above):
        for rotation in range(3):
            c = ORDERS[rotation][2]
            shared[rotation, where][0].wait_recv()
            multiply(other, rotation, {c: where(c)})
    for rotation in range(3):
        c = ORDERS[rotation][2]
        multiply(core, rotation, {c: across(c)})
    for rotation in range(3):
        c = ORDERS[rotation][2]
        for copy in shared[rotation, across]:
            copy.wait_recv()
        multiply(other, rotation, {c: across(c)})

    expert = (pos["z"] * 2 + x_lo) * 4 + pos["y"]
    parts = rows[0, :, :, :, :, HALF : HALF + 128].astype(jnp.float32).reshape(512, 128)
    lane = lax.broadcasted_iota(jnp.int32, parts.shape, 1)
    picked = jnp.where((lane == expert) | (lane == expert + 32), parts, 0.0)
    row_gate = jnp.sum(picked, axis=1, keepdims=True)
    gate_part = gate_acc[...].reshape(512, 256)
    active[core] = (gate_part * jax.nn.sigmoid(gate_part) * up_acc[...].reshape(512, 256) * row_gate).astype(
        jnp.bfloat16
    )

    handed["active"] = send(active.at[core], active.at[core], partner)
    loads["down"].wait()
    handed["down"].wait_recv()
    handed["active"].wait_recv()

    def mix_block(rotation, phase):
        dims = ORDERS[rotation][::-1]

        def block(place, cols):
            at = {}
            for earlier in dims[:phase]:
                at[earlier] = pos[earlier]
            at[dims[phase]] = place
            return mix_sum.at[
                at.get("x", slice(None)),
                at.get("y", slice(None)),
                at.get("z", slice(None)),
                slice(None),
                span(cols),
            ]

        return block

    def mix_land(rotation, phase):
        land = (mix_land0, mix_land1, mix_land2)[phase]

        def place(slot, cols):
            return land.at[
                (rotation, slot) + (slice(None),) * (3 - phase) + (pl.ds(0, cols[1]),)
            ]

        return place

    subs = {"across": across, "below": below, "above": above, "own": lambda dim: pos[dim]}
    order = tuple(subs)
    started, relayed = {}, {}

    def sub_block(rotation, name):
        b, c = ORDERS[rotation][1:]

        def block(where, cols):
            at = {c: where, b: subs[name](b)}
            index = tuple(at.get(dim, slice(None)) for dim in ("x", "y", "z"))
            return mix_sum.at[index + (slice(None), span(cols))]

        def land(slot, cols):
            at = {b: subs[name](b)}
            index = tuple(at.get(dim, slice(None)) for dim in ("x", "y", "z") if dim != c)
            return mix_land0.at[(rotation, slot) + index + (slice(None), pl.ds(0, cols[1]))]

        return c, block, land, MIX_COLS[rotation]

    def sub_relayed_part(rotation, name, part):
        dim, block, land, cols = sub_block(rotation, name)
        way = above(dim) if part == 0 else below(dim)
        piece = block(across(dim), cols[part])
        return send(piece, land(2 * part, cols[part]), device(dim, way))

    def sub_direct_part(rotation, name, part):
        dim, block, land, cols = sub_block(rotation, name)
        way = below(dim) if part == 0 else above(dim)
        piece = block(way, cols[part])
        return send(piece, land(2 * part + 1, cols[part]), device(dim, way))

    def sub_finish(rotation, name):
        dim, block, land, cols = sub_block(rotation, name)
        begun = tuple(started[rotation, name, part] for part in range(2))
        ring_finish(dim, block, land, cols, begun, relayed[rotation, name], keep_in(block, dim))

    for rotation in range(3):
        for part in range(2):
            cols = MIX_COLS[rotation][part]
            for start in range(cols[0], cols[0] + cols[1], UNIT):
                width = min(UNIT, cols[0] + cols[1] - start)
                piece = pl.ds(start, width)
                share = jnp.dot(
                    active[0], w_down[0:256, piece], preferred_element_type=jnp.float32
                ) + jnp.dot(active[1], w_down[256:512, piece], preferred_element_type=jnp.float32)
                mix_sum[:, :, :, :, piece] = share.reshape(4, 4, 4, 8, width).astype(jnp.bfloat16)
            for name in order:
                started[rotation, name, part] = [sub_relayed_part(rotation, name, part)]
            started[rotation, "across", part].append(sub_direct_part(rotation, "across", part))

    middle = {}
    for number, name in enumerate(order):
        for rotation in range(3):
            dim, block, land, cols = sub_block(rotation, name)
            begun = tuple(started[rotation, name, part] for part in range(2))
            relayed[rotation, name] = ring_relay(dim, block, land, cols, begun)
            if number < 3:
                for part in range(2):
                    started[rotation, order[number + 1], part].append(
                        sub_direct_part(rotation, order[number + 1], part)
                    )
        if number == 0:
            continue
        ready = order[number - 1]
        for rotation in range(3):
            sub_finish(rotation, ready)
            b = ORDERS[rotation][1]
            block, land = mix_block(rotation, 1), mix_land(rotation, 1)
            first, second = MIX_COLS[rotation]
            up, down = device(b, above(b)), device(b, below(b))
            if ready == "across":
                middle[rotation] = (
                    [send(block(across(b), first), land(0, first), up)],
                    [send(block(across(b), second), land(2, second), down)],
                )
            elif ready == "below":
                middle[rotation][0].append(send(block(below(b), first), land(1, first), down))
            else:
                middle[rotation][1].append(send(block(above(b), second), land(3, second), up))
    for rotation in range(3):
        relayed[rotation] = ring_relay(
            ORDERS[rotation][1],
            mix_block(rotation, 1),
            mix_land(rotation, 1),
            MIX_COLS[rotation],
            middle[rotation],
        )
    for rotation in range(3):
        sub_finish(rotation, "own")
    for rotation in range(3):
        dim = ORDERS[rotation][1]
        block = mix_block(rotation, 1)
        ring_finish(
            dim,
            block,
            mix_land(rotation, 1),
            MIX_COLS[rotation],
            middle[rotation],
            relayed[rotation],
            keep_in(block, dim),
        )
        started[rotation] = direct_start(
            ORDERS[rotation][0],
            mix_block(rotation, 2),
            mix_land(rotation, 2),
            whole_cols(MIX_COLS[rotation]),
        )

    def add_to_stream(cols, total):
        stream[:, span(cols)] += total

    for rotation in range(3):
        direct_finish(
            ORDERS[rotation][0],
            mix_block(rotation, 2),
            mix_land(rotation, 2),
            whole_cols(MIX_COLS[rotation]),
            started[rotation],
            add_to_stream,
        )
    top, bottom = stream[0:4, :], stream[4:8, :]
    swap_out[...] = jnp.where(first_core, bottom, top)
    swapped = send(swap_out, swap_in, partner)
    mine = jnp.where(first_core, top, bottom)
    swapped.wait_recv()
    theirs = swap_in[...]
    out_ref[:, 0:HALF] = jnp.where(first_core, mine, theirs).astype(jnp.bfloat16)
    out_ref[:, HALF : 2 * HALF] = jnp.where(first_core, theirs, mine).astype(jnp.bfloat16)
    for copy in sent:
        copy.wait_send()
    for pair in range(2):
        latent_copies(pair).wait_send()


def layer(
    lengths,
    residual,
    norm_gain,
    expert_ids,
    gate_values,
    query_latent,
    query_rope,
    cache_latent,
    cache_rope,
    value_up,
    out_proj,
    w_gate,
    w_up,
    w_down,
):
    bf16, f32 = jnp.bfloat16, jnp.float32
    vmem = pl.BlockSpec(memory_space=pltpu.VMEM)
    hbm = pl.BlockSpec(memory_space=pl.ANY)
    return pl.pallas_call(
        layer_kernel,
        out_shape=jax.ShapeDtypeStruct((4, 2 * HALF), bf16),
        in_specs=[pl.BlockSpec(memory_space=pltpu.SMEM)] + [vmem] * 4 + [hbm] * 9,
        out_specs=vmem,
        scratch_shapes=[
            pltpu.VMEM(query_latent.shape, bf16),
            pltpu.VMEM(query_rope.shape, bf16),
            pltpu.VMEM((2, 2048, 512), bf16),
            pltpu.VMEM(cache_rope.shape, bf16),
            pltpu.VMEM((128, 2048), f32),
            pltpu.VMEM((128, 2048), bf16),
            pltpu.VMEM((64, 4, 512), f32),
            pltpu.VMEM((2, 64, 4, 512), bf16),
            pltpu.VMEM((2, 64, 4, 512), bf16),
            pltpu.VMEM(value_up.shape, bf16),
            pltpu.VMEM((256, 128), f32),
            pltpu.VMEM((256, 128), f32),
            pltpu.VMEM((32, 8, 128), f32),
            pltpu.VMEM((32, 8, 128), f32),
            pltpu.VMEM((512, HALF), bf16),
            pltpu.VMEM(w_gate.shape, bf16),
            pltpu.VMEM(w_up.shape, bf16),
            pltpu.VMEM((512, HALF), bf16),
            pltpu.VMEM((2, 256, 256), bf16),
            pltpu.VMEM((4, 2, 4, 8, HALF), bf16),
            pltpu.VMEM((6, 2, 4, 8, 1024), bf16),
            pltpu.VMEM((6, 4, 2, 8, 1024), bf16),
            pltpu.VMEM((2, 3, 2, 8, 1792), bf16),
            pltpu.VMEM((8, HALF), bf16),
            pltpu.VMEM((4, HALF), bf16),
            pltpu.VMEM((4, HALF), bf16),
            pltpu.VMEM((4, 128), f32),
            pltpu.VMEM((4, 128), f32),
            pltpu.VMEM((8, 128), f32),
            pltpu.VMEM((8, 128), f32),
            pltpu.VMEM((8, HALF), f32),
            pltpu.VMEM((4, HALF), f32),
            pltpu.VMEM((4, HALF), f32),
            pltpu.VMEM((2, 4, 4, 4, 8, HALF + 128), bf16),
            pltpu.VMEM((4, 4, 4, 8, 256), f32),
            pltpu.VMEM((4, 4, 4, 8, 256), f32),
            pltpu.VMEM((2, 512, 256), bf16),
            pltpu.VMEM((4, 4, 4, 8, HALF), bf16),
            pltpu.VMEM((3, 6, 4, 4, 8, 768), bf16),
            pltpu.VMEM((3, 6, 4, 8, 768), bf16),
            pltpu.VMEM((3, 3, 8, 1280), bf16),
            pltpu.SemaphoreType.DMA((2,)),
            pltpu.SemaphoreType.DMA((8,)),
            pltpu.SemaphoreType.DMA((2,)),
            pltpu.SemaphoreType.DMA((2,)),
            pltpu.SemaphoreType.DMA((260,)),
            pltpu.SemaphoreType.DMA((260,)),
        ],
        compiler_params=pltpu.CompilerParams(
            collective_id=0, has_side_effects=True, vmem_limit_bytes=63 * 1024 * 1024
        ),
    )(
        lengths,
        residual,
        norm_gain,
        expert_ids,
        gate_values,
        query_latent,
        query_rope,
        cache_latent,
        cache_rope,
        value_up,
        out_proj,
        w_gate,
        w_up,
        w_down,
    )


def local(
    query_latent,
    query_rope,
    cache_latent,
    cache_rope,
    lengths,
    value_up,
    out_proj,
    residual,
    norm_gain,
    expert_ids,
    gate_values,
    w_gate,
    w_up,
    w_down,
):
    return layer(
        lengths,
        residual,
        norm_gain[None, :],
        expert_ids,
        gate_values,
        query_latent,
        jnp.swapaxes(query_rope, 1, 2),
        cache_latent,
        cache_rope,
        value_up,
        out_proj,
        w_gate[0],
        w_up[0],
        w_down[0],
    )


def solution(mesh):
    finer = Mesh(
        mesh.devices.reshape(mesh.shape["group"], 4, 2, 4, 2),
        ("group", "dev_0", "dev_1", "dev_2", "dev_3"),
    )
    return jax.shard_map(
        local,
        mesh=finer,
        in_specs=(
            P(GROUP_DEV, None, None),
            P(GROUP_DEV, None, None),
            P(GROUP_DEV, None, None),
            P(GROUP_DEV, None, None),
            P(GROUP_DEV),
            P(DEV, None, None),
            P(DEV, None),
            P(GROUP_DEV, None),
            P(),
            P(GROUP_DEV, None),
            P(GROUP_DEV, None),
            P(DEV, None, "group"),
            P(DEV, None, "group"),
            P(DEV, "group", None),
        ),
        out_specs=P(GROUP_DEV, None),
        check_vma=False,
    )
```
